256 devices in a mesh: seq: 64 (over z_lo, x, y), batch: 4 (over z_hi, core).
Axes of the slice: x: 4, y: 4, z: 8 (z_hi: 2, z_lo: 4; z = z_hi * 4 + z_lo), core: 2. Of those that a mesh axis runs over, the one named last changes fastest.
Arguments:
- inputs: bfloat16 [4, 16384, 2048], P('batch', 'seq'), may hold values from -106.50967 to 106.50967
- output_grad: bfloat16 [4, 16384, 2048], P('batch', 'seq'), may hold values from -6 to 6
- norm_gain: float32 [2048], replicated, may hold values from 0.1 to 1.9
- gate_bias: float32 [2048], P('seq'), as said below
- state_in: float32 [4, 2048], P('batch', 'seq'), may hold values from -6 to 6
- w_gate: bfloat16 [2048, 2048], P('seq'), may hold values from -0.44194174 to 0.44194174
- w_cand: bfloat16 [2048, 2048], P('seq'), may hold values from -0.125 to 0.125
- w_out: bfloat16 [2048, 2048], P('seq'), may hold values from -0.125 to 0.125
Outputs:
- layer_out: bfloat16 [4, 16384, 2048], P('batch', 'seq')
- input_grad: bfloat16 [4, 16384, 2048], P('batch', 'seq')
- state_grad: float32 [4, 2048], P('batch', 'seq')
- bias_grad: float32 [2048], P('seq')
The draws below stay inside these ranges and needn't reach their ends.
Inputs may be any that keep to these rules, and one draw needn't show every extreme that they name: `gate_bias`: every value is at least -ln(16384) - 1.5.
All inputs are finite; a program needn't handle non-finite values.
Results may differ from the reference program's by a relative error of at most 0.013.
Values may be sent and summed in bfloat16 or wider, within the bound.
A program may use at most 128 MiB of HBM per device.

```python
import math
from functools import partial
import jax
import jax.numpy as jnp
from jax import lax

MODEL_WIDTH = 2048
H = 2048
BATCH_SEQUENCES = 4
WINDOW_TOKENS = 16384


def rate_plan(key):
    folded = jax.random.fold_in(key, 7)
    key_fast, key_slow, key_quick, key_aim = jax.random.split(folded, 4)
    fast_share = 0.5
    fast_flag = jax.random.uniform(key_fast, (H,)) < fast_share
    slow_bias = -math.log(WINDOW_TOKENS) - jax.random.uniform(key_slow, (H,), minval=0.2, maxval=1.5)
    quick_bias = jax.random.uniform(key_quick, (H,), minval=-4.3, maxval=-3.3)
    bias_values = jnp.where(fast_flag, quick_bias, slow_bias)
    lift_values = (-bias_values - 1.1) / math.sqrt(MODEL_WIDTH)
    target_vector = jax.random.normal(key_aim, (MODEL_WIDTH,))
    target_vector = target_vector / jnp.sqrt(jnp.sum(target_vector * target_vector))
    return (bias_values, lift_values, target_vector)


def draw_gate_bias(key, part):
    bias_values, lift_values, target_vector = rate_plan(key)
    return bias_values.astype(jnp.float32)


def draw_w_gate(key, part):
    bias_values, lift_values, target_vector = rate_plan(key)
    base_sample = jax.random.normal(jax.random.fold_in(key, 11), (MODEL_WIDTH, H))
    base_sample = jnp.clip(base_sample, -6.0, 6.0) / math.sqrt(MODEL_WIDTH)
    return (base_sample + target_vector[:, None] * lift_values[None, :]).astype(jnp.bfloat16)


def draw_inputs(key, part):
    bias_values, lift_values, target_vector = rate_plan(key)
    key_base = jax.random.fold_in(key, 13)
    key_positions = jax.random.fold_in(key, 17)
    base_sample = jnp.clip(jax.random.normal(key_base, (BATCH_SEQUENCES, WINDOW_TOKENS, MODEL_WIDTH)), -6.0, 6.0)
    spike_positions = jax.random.randint(key_positions, (BATCH_SEQUENCES, 3), 0, WINDOW_TOKENS)
    flagged_entries = jnp.any(jnp.arange(WINDOW_TOKENS)[None, :, None] == spike_positions[:, None, :], axis=-1)
    spike_rows = 0.1 * base_sample + 2.0 * math.sqrt(MODEL_WIDTH) * target_vector
    return jnp.where(flagged_entries[:, :, None], spike_rows, base_sample).astype(jnp.bfloat16)


def levels(rng, dims, cuts, low, top_value):
    loudness, own = 1.0, jax.random.fold_in(rng, 6)
    for position, blocks in cuts:
        draws = jnp.exp(jax.random.uniform(jax.random.fold_in(own, position), (blocks,), jnp.float32, low / len(cuts), top_value / len(cuts)))
        loudness = loudness * jnp.repeat(draws, dims[position] // blocks).reshape([-1 if axis == position else 1 for axis in range(len(dims))])
    return loudness


def gaussian(key, extent, scale, bound, shards=(), dtype=jnp.bfloat16):
    values = jax.random.normal(key, extent, jnp.float32) * scale
    if len(shards) > 0:
        values = levels(key, extent, shards, -0.22, 0.18) * values
    return jnp.clip(values, min=-bound, max=bound).astype(dtype)


def setup_inputs(seed: int = 0) -> dict:
    seeds = jax.random.split(jax.random.key(seed), 9)
    inputs = draw_inputs(jax.random.fold_in(seeds[8], 71), 0)
    output_grad = gaussian(seeds[1], (BATCH_SEQUENCES, WINDOW_TOKENS, MODEL_WIDTH), 1.0, 6.0, ((0, 4), (1, 64)))
    norm_gain = jnp.clip(1.0 + 0.18 * jax.random.normal(seeds[2], (MODEL_WIDTH,), jnp.float32), 0.1, 1.9)
    gate_bias = draw_gate_bias(jax.random.fold_in(seeds[8], 71), 0)
    state_in = gaussian(seeds[4], (BATCH_SEQUENCES, H), 1.0, 6.0, ((0, 4), (1, 64)), jnp.float32)
    w_gate = draw_w_gate(jax.random.fold_in(seeds[8], 71), 0)
    w_cand = gaussian(seeds[6], (MODEL_WIDTH, H), MODEL_WIDTH ** -0.5, 0.125, ((0, 64),))
    w_out = gaussian(seeds[7], (H, MODEL_WIDTH), H ** -0.5, 0.125, ((0, 64),))
    return {"inputs": inputs, "output_grad": output_grad, "norm_gain": norm_gain, "gate_bias": gate_bias, "state_in": state_in, "w_gate": w_gate, "w_cand": w_cand, "w_out": w_out}


EPSILON = 1e-06

def compose(earlier, later):
    return (earlier[0] * later[0], later[0] * earlier[1] + later[1])

def one_sequence(norm_gain, gate_bias, w_gate, w_cand, w_out, operands):
    seq_tokens, seq_grads, initial = operands
    residual = seq_tokens.astype(jnp.float32)
    mean_square = lax.optimization_barrier(jnp.mean(residual * residual, axis=-1, keepdims=True))
    inverse_rms = lax.rsqrt(mean_square + EPSILON)
    unit_rows = residual * inverse_rms
    normed = (unit_rows * norm_gain).astype(jnp.bfloat16)
    gate_pre = jnp.dot(normed, w_gate, preferred_element_type=jnp.float32).astype(jnp.bfloat16)
    cand_pre = jnp.dot(normed, w_cand, preferred_element_type=jnp.float32).astype(jnp.bfloat16)
    gate_input = gate_pre.astype(jnp.float32) + gate_bias
    update = jax.nn.sigmoid(gate_input)
    retain = jax.nn.sigmoid(-gate_input)
    candidate = cand_pre.astype(jnp.float32)
    drive_term = (update * candidate).at[0].add(retain[0] * initial)
    _, states = lax.associative_scan(compose, (retain, drive_term), axis=0)
    state_rows = states.astype(jnp.bfloat16)
    mixed_rows = (residual + jnp.dot(state_rows, w_out, preferred_element_type=jnp.float32)).astype(jnp.bfloat16)
    back_grads = jnp.dot(seq_grads, w_out.T, preferred_element_type=jnp.float32).astype(jnp.bfloat16)
    next_retain = jnp.concatenate([retain[1:], jnp.zeros((1, retain.shape[1]), jnp.float32)], axis=0)
    _, carried = lax.associative_scan(compose, (next_retain, back_grads.astype(jnp.float32)), axis=0, reverse=True)
    first_grad = retain[0] * carried[0]
    earlier_states = jnp.concatenate([initial[None, :], states[:-1]], axis=0)
    gate_grad = carried * (candidate - earlier_states) * update * retain
    cand_grad = carried * update
    bias_terms = lax.optimization_barrier(jnp.sum(gate_grad, axis=0))
    normed_grad = jnp.dot(gate_grad.astype(jnp.bfloat16), w_gate.T, preferred_element_type=jnp.float32)
    normed_grad = normed_grad + jnp.dot(cand_grad.astype(jnp.bfloat16), w_cand.T, preferred_element_type=jnp.float32)
    unit_grad = normed_grad * norm_gain
    input_rows = inverse_rms * (unit_grad - unit_rows * lax.optimization_barrier(jnp.mean(unit_grad * unit_rows, axis=-1, keepdims=True)))
    token_grad = (seq_grads.astype(jnp.float32) + input_rows).astype(jnp.bfloat16)
    return (mixed_rows, token_grad, first_grad, bias_terms)

def reference(inputs, output_grad, norm_gain, gate_bias, state_in, w_gate, w_cand, w_out):
    worker = partial(one_sequence, norm_gain, gate_bias, w_gate, w_cand, w_out)
    layer_out, input_grad, state_grad, bias_terms = lax.map(worker, (inputs, output_grad, state_in))
    return (layer_out, input_grad, state_grad, lax.optimization_barrier(jnp.sum(bias_terms, axis=0)))
```

```python
import functools
import jax
import jax.numpy as jnp
from jax import lax
from jax.sharding import PartitionSpec as P
from jax.experimental import pallas as pl
from jax.experimental.pallas import tpu as pltpu

EPSILON = 1e-06
MESH = pl.DeviceIdType.MESH
ORDERS = ("yxz", "zyx", "xzy")
AXIS_DIM = {"z": 0, "x": 1, "y": 2}
CHUNKS = 2


class Place:
    def __init__(self):
        seq = lax.axis_index("seq")
        batch = lax.axis_index("batch")
        self.seq, self.batch = seq, batch
        self.at = {"z": seq // 16, "x": lax.rem(seq // 4, 4), "y": lax.rem(seq, 4)}
        self.z_hi = batch // 2
        self.core = lax.rem(batch, 2)

    def device(self, z, x, y, z_hi, core):
        return (z * 16 + x * 4 + y, z_hi * 2 + core)

    def ring(self, axis, step):
        z, x, y = self.at["z"], self.at["x"], self.at["y"]
        if axis == "x":
            return self.device(z, lax.rem(x + 4 + step, 4), y, self.z_hi, self.core)
        if axis == "y":
            return self.device(z, x, lax.rem(y + 4 + step, 4), self.z_hi, self.core)
        full = lax.rem(self.z_hi * 4 + z + 8 + step, 8)
        return self.device(lax.rem(full, 4), x, y, full // 4, self.core)

    def sibling(self):
        return (self.seq, self.z_hi * 2 + 1 - self.core)


def gather_kernel(
    gate_ref, cand_ref, out_ref, full_ref, weights, own_sem, send_sem, recv_sem, sib_send, sib_recv, put_sem
):
    place = Place()
    core = place.core
    shards = (out_ref, gate_ref, cand_ref)
    own = []
    for w in range(3):
        for half in range(2):
            copy = pltpu.make_async_copy(
                shards[w].at[pl.ds(16 * half, 16), :],
                weights.at[w, place.at["z"], place.at["x"], place.at["y"], half],
                own_sem.at[w, half],
            )
            copy.start()
            own.append(copy)
    barrier = pltpu.get_barrier_semaphore()
    peers = [place.ring(a, d) for a in "xyz" for d in (1, -1)] + [place.sibling()]
    for peer in peers:
        pl.semaphore_signal(barrier, inc=1, device_id=peer, device_id_type=MESH)
    pl.semaphore_wait(barrier, len(peers))
    for copy in own:
        copy.wait()

    def slab(w, phase, step, which, cols):
        order = ORDERS[w]
        index = [None, None, None]
        for position, axis in enumerate(order):
            own_at = place.at[axis]
            if position < phase:
                index[AXIS_DIM[axis]] = slice(None)
            elif position == phase:
                index[AXIS_DIM[axis]] = lax.rem(own_at + 4 + step, 4)
            else:
                index[AXIS_DIM[axis]] = own_at
        return weights.at[w, index[0], index[1], index[2], which, :, pl.ds(cols[0], cols[1])]

    def chunks(phase):
        n = CHUNKS if phase == 2 else 1
        return [(q, (2048 // n * q, 2048 // n)) for q in range(n)]

    def piece(w, phase, kind, cols, outgoing):
        right = kind % 2 == 0
        if kind < 2:
            span = cols
            step = 0 if outgoing else (-1 if right else 1)
        else:
            span = (cols[0], cols[1] // 2) if right else (cols[0] + cols[1] // 2, cols[1] // 2)
            step = (-1 if right else 1) if outgoing else 2
        return step, span

    def send(w, phase, kind, q, cols):
        step, span = piece(w, phase, kind, cols, True)
        ref = slab(w, phase, step, core, span)
        return pltpu.make_async_remote_copy(
            src_ref=ref, dst_ref=ref,
            send_sem=send_sem.at[w, phase, kind, q], recv_sem=recv_sem.at[w, phase, kind, q],
            device_id=place.ring(ORDERS[w][phase], 1 if kind % 2 == 0 else -1), device_id_type=MESH,
        )

    def arrival(w, phase, kind, q, cols):
        step, span = piece(w, phase, kind, cols, False)
        ref = slab(w, phase, step, core, span)
        return pltpu.make_async_remote_copy(
            src_ref=ref, dst_ref=ref,
            send_sem=send_sem.at[w, phase, kind, q], recv_sem=recv_sem.at[w, phase, kind, q],
            device_id=place.ring(ORDERS[w][phase], 1 if kind % 2 == 0 else -1), device_id_type=MESH,
        )

    def share(w, phase, kind, q, cols, mine):
        step, span = piece(w, phase, kind, cols, False)
        ref = slab(w, phase, step, core if mine else 1 - core, span)
        return pltpu.make_async_remote_copy(
            src_ref=ref, dst_ref=ref,
            send_sem=sib_send.at[w, phase, kind, q], recv_sem=sib_recv.at[w, phase, kind, q],
            device_id=place.sibling(), device_id_type=MESH,
        )

    for phase in range(3):
        for q, cols in chunks(phase):
            for w in range(3):
                for kind in (0, 1):
                    send(w, phase, kind, q, cols).start()
        for q, cols in chunks(phase):
            for w in range(3):
                for kind in (0, 1):
                    arrival(w, phase, kind, q, cols).wait_recv()
                    send(w, phase, kind + 2, q, cols).start()
                    share(w, phase, kind, q, cols, True).start()
        for q, cols in chunks(phase):
            for w in range(3):
                for kind in (2, 3):
                    arrival(w, phase, kind, q, cols).wait_recv()
                    share(w, phase, kind, q, cols, True).start()
    for phase in range(3):
        for q, cols in chunks(phase):
            for w in range(3):
                for kind in range(4):
                    share(w, phase, kind, q, cols, False).wait_recv()
                    share(w, phase, kind, q, cols, True).wait_send()
                    send(w, phase, kind, q, cols).wait_send()
    put = pltpu.make_async_copy(weights, full_ref, put_sem)
    put.start()
    put.wait()


def gather_weights(w_gate, w_cand, w_out):
    full = pl.pallas_call(
        gather_kernel,
        out_shape=jax.ShapeDtypeStruct((3, 4, 4, 4, 2, 16, 2048), jnp.bfloat16),
        in_specs=[pl.BlockSpec(memory_space=pltpu.VMEM)] * 3,
        out_specs=pl.BlockSpec(memory_space=pl.ANY),
        scratch_shapes=[
            pltpu.VMEM((3, 4, 4, 4, 2, 16, 2048), jnp.bfloat16),
            pltpu.SemaphoreType.DMA((3, 2)),
            pltpu.SemaphoreType.DMA((3, 3, 4, CHUNKS)),
            pltpu.SemaphoreType.DMA((3, 3, 4, CHUNKS)),
            pltpu.SemaphoreType.DMA((3, 3, 4, CHUNKS)),
            pltpu.SemaphoreType.DMA((3, 3, 4, CHUNKS)),
            pltpu.SemaphoreType.DMA,
        ],
        compiler_params=pltpu.CompilerParams(collective_id=0, has_side_effects=True, vmem_limit_bytes=60 * 1024 * 1024),
        name="weights",
    )(w_gate, w_cand, w_out)
    full = full.reshape(3, 2048, 2048)
    return full[1], full[2], full[0]


def shifted(values, axis, offset, fill, reverse):
    length = values.shape[axis]
    pad_shape = list(values.shape)
    pad_shape[axis] = offset
    padding = jnp.full(tuple(pad_shape), fill, values.dtype)
    if reverse:
        kept = lax.slice_in_dim(values, offset, length, 1, axis)
        return jnp.concatenate([kept, padding], axis=axis)
    kept = lax.slice_in_dim(values, 0, length - offset, 1, axis)
    return jnp.concatenate([padding, kept], axis=axis)


def shift_scan(keep, drive, axis, reverse):
    length = keep.shape[axis]
    offset = 1
    while offset < length:
        keep_far = shifted(keep, axis, offset, 1.0, reverse)
        drive_far = shifted(drive, axis, offset, 0.0, reverse)
        drive = keep * drive_far + drive
        keep = keep * keep_far
        offset = offset * 2
    return (keep, drive)


def on_device(inputs, output_grad, norm_gain, gate_bias, state_in, w_gate, w_cand, w_out):
    token_rows = inputs[0]
    grad_rows = output_grad[0]
    seq = lax.axis_index("seq")
    gate_full, cand_full, out_full = gather_weights(w_gate, w_cand, w_out)
    bias_full = lax.all_gather(gate_bias, "seq", axis=0, tiled=True)
    initial_full = lax.all_gather(state_in[0], "seq", axis=0, tiled=True)
    residual = token_rows.astype(jnp.float32)
    mean_square = jnp.mean(residual * residual, axis=-1, keepdims=True)
    inverse_rms = lax.rsqrt(mean_square + EPSILON)
    unit_rows = residual * inverse_rms
    normed = (unit_rows * norm_gain).astype(jnp.bfloat16)
    gate_pre = jnp.dot(normed, gate_full, preferred_element_type=jnp.float32).astype(jnp.bfloat16)
    cand_pre = jnp.dot(normed, cand_full, preferred_element_type=jnp.float32).astype(jnp.bfloat16)
    back = lax.dot_general(
        grad_rows, out_full, (((1,), (1,)), ((), ())), preferred_element_type=jnp.float32
    ).astype(jnp.bfloat16).astype(jnp.float32)
    gate_input = gate_pre.astype(jnp.float32) + bias_full
    update = jax.nn.sigmoid(gate_input)
    retain = jax.nn.sigmoid(-gate_input)
    candidate = cand_pre.astype(jnp.float32)
    reach, local_states = shift_scan(retain, update * candidate, 0, False)
    tail_reach, local_carry = shift_scan(retain, retain * back, 0, True)
    summary = jnp.stack([reach[-1], local_states[-1], local_carry[0]])
    every = lax.all_gather(summary, "seq", axis=0)
    keeps, ends, carries = every[:, 0], every[:, 1], every[:, 2]
    ends = ends.at[0].add(keeps[0] * initial_full)
    _, prefix = shift_scan(keeps, ends, 0, False)
    _, suffix = shift_scan(keeps, carries, 0, True)
    entering = jnp.where(seq == 0, initial_full, prefix[jnp.maximum(seq - 1, 0)])
    leaving = jnp.where(seq == 63, 0.0, suffix[jnp.minimum(seq + 1, 63)])
    state_grad = lax.dynamic_slice(suffix[0], (seq * 32,), (32,))
    states = local_states + reach * entering
    earlier = jnp.concatenate([entering[None], states[:-1]], axis=0)
    scaled = local_carry + tail_reach * leaving
    carried = back + jnp.concatenate([scaled[1:], leaving[None]], axis=0)
    gate_grad = carried * (candidate - earlier) * update * retain
    cand_grad = carried * update
    bias_part = jnp.sum(gate_grad, axis=0)
    layer_rows = (
        residual + jnp.dot(states.astype(jnp.bfloat16), out_full, preferred_element_type=jnp.float32)
    ).astype(jnp.bfloat16)
    back_dims = (((1,), (1,)), ((), ()))
    normed_grad = lax.dot_general(
        gate_grad.astype(jnp.bfloat16), gate_full, back_dims, preferred_element_type=jnp.float32
    ) + lax.dot_general(
        cand_grad.astype(jnp.bfloat16), cand_full, back_dims, preferred_element_type=jnp.float32
    )
    unit_grad = normed_grad * norm_gain
    input_rows = inverse_rms * (
        unit_grad - unit_rows * jnp.mean(unit_grad * unit_rows, axis=-1, keepdims=True)
    )
    token_grad = (grad_rows.astype(jnp.float32) + input_rows).astype(jnp.bfloat16)
    bias_grad = lax.psum(lax.psum_scatter(bias_part, "seq", scatter_dimension=0, tiled=True), "batch")
    return (layer_rows[None], token_grad[None], state_grad[None], bias_grad)


def solution(mesh):
    return jax.shard_map(
        on_device,
        mesh=mesh,
        in_specs=(
            P("batch", "seq", None),
            P("batch", "seq", None),
            P(),
            P("seq"),
            P("batch", "seq"),
            P("seq", None),
            P("seq", None),
            P("seq", None),
        ),
        out_specs=(P("batch", "seq", None), P("batch", "seq", None), P("batch", "seq"), P("seq")),
        check_vma=False,
    )
```

```python
import jax
import jax.numpy as jnp
from jax import lax
from jax.sharding import PartitionSpec as P
from jax.experimental import pallas as pl
from jax.experimental.pallas import tpu as pltpu

EPSILON = 1e-06
MESH = pl.DeviceIdType.MESH
ORDERS = ("yxz", "zyx", "xzy")
AXIS_DIM = {"z": 0, "x": 1, "y": 2}
CHUNKS = 4
TOKENS = 256
WIDTH = 2048
SPAN = WIDTH // CHUNKS
BLOCK = 256
STEPS = TOKENS // 8
LANES = 512
F32 = jnp.float32
BF16 = jnp.bfloat16
NT = (((1,), (1,)), ((), ()))


class Place:
    def __init__(self):
        seq = lax.axis_index("seq")
        batch = lax.axis_index("batch")
        self.seq, self.batch = seq, batch
        self.at = {"z": seq // 16, "x": lax.rem(seq // 4, 4), "y": lax.rem(seq, 4)}
        self.z_hi = batch // 2
        self.core = lax.rem(batch, 2)

    def device(self, z, x, y, z_hi, core):
        return (z * 16 + x * 4 + y, z_hi * 2 + core)

    def line(self, axis, step):
        at = dict(self.at)
        at[axis] = lax.rem(at[axis] + 4 + step, 4)
        return self.device(at["z"], at["x"], at["y"], self.z_hi, self.core)

    def column(self, step, flip):
        full = lax.rem(self.z_hi * 4 + self.at["z"] + 8 + step, 8)
        core = lax.rem(self.core + flip, 2)
        return self.device(lax.rem(full, 4), self.at["x"], self.at["y"], full // 4, core)

    def ring(self, axis, step):
        return self.column(step, 0) if axis == "z" else self.line(axis, step)

    def sibling(self):
        return self.column(0, 1)


def remote(src, dst, send_sem, recv_sem, device):
    return pltpu.make_async_remote_copy(
        src_ref=src, dst_ref=dst, send_sem=send_sem, recv_sem=recv_sem, device_id=device, device_id_type=MESH
    )


class Weights:
    def __init__(self, place, buffer, send_sem, recv_sem, sib_send, sib_recv):
        self.place, self.buffer = place, buffer
        self.sems, self.sib_sems = (send_sem, recv_sem), (sib_send, sib_recv)

    def slab(self, w, phase, step, which, q, part):
        index = [None, None, None]
        for position, axis in enumerate(ORDERS[w]):
            own_at = self.place.at[axis]
            if position < phase:
                index[AXIS_DIM[axis]] = slice(None)
            elif position == phase:
                index[AXIS_DIM[axis]] = lax.rem(own_at + 4 + step, 4)
            else:
                index[AXIS_DIM[axis]] = own_at
        start, width = 0, WIDTH
        if phase == 2 and w == 0:
            index[AXIS_DIM["x"]] = q
        elif phase == 2:
            start, width = q * SPAN, SPAN
        if part is not None:
            width = width // 2
            start = start + part * width
        return self.buffer.at[w, index[0], index[1], index[2], which, :, pl.ds(start, width)]

    def piece(self, w, phase, kind, q, which, outgoing):
        right = kind % 2 == 0
        if kind < 2:
            step, part = (0 if outgoing else (-1 if right else 1)), None
        else:
            step, part = ((-1 if right else 1) if outgoing else 2), kind - 2
        return self.slab(w, phase, step, which, q, part)

    def hop(self, w, phase, kind, q, outgoing):
        ref = self.piece(w, phase, kind, q, self.place.core, outgoing)
        device = self.place.ring(ORDERS[w][phase], 1 if kind % 2 == 0 else -1)
        at = (w, phase, kind, q)
        return remote(ref, ref, self.sems[0].at[at], self.sems[1].at[at], device)

    def share(self, w, phase, kind, q, mine):
        ref = self.piece(w, phase, kind, q, self.place.core if mine else 1 - self.place.core, False)
        at = (w, phase, kind, q)
        return remote(ref, ref, self.sib_sems[0].at[at], self.sib_sems[1].at[at], self.place.sibling())

    def open(self, phase, q):
        for w in range(3):
            for kind in (0, 1):
                self.hop(w, phase, kind, q, True).start()

    def near(self, phase, q):
        for w in range(3):
            for kind in (0, 1):
                self.hop(w, phase, kind, q, False).wait_recv()
                self.hop(w, phase, kind + 2, q, True).start()
                self.share(w, phase, kind, q, True).start()

    def far(self, phase, q):
        for w in range(3):
            for kind in (2, 3):
                self.hop(w, phase, kind, q, False).wait_recv()
                self.share(w, phase, kind, q, True).start()

    def shared(self, w, phase, q):
        for kind in range(4):
            self.share(w, phase, kind, q, False).wait_recv()

    def drain(self, phase, q):
        for w in range(3):
            for kind in range(4):
                self.hop(w, phase, kind, q, True).wait_send()
                self.share(w, phase, kind, q, True).wait_send()


class LineExchange:
    def __init__(self, place, axis, ref_of, send_sem, recv_sem, level):
        self.place, self.axis, self.ref_of = place, axis, ref_of
        self.sems, self.level = (send_sem, recv_sem), level

    def copy(self, step, outgoing):
        at = self.place.at[self.axis]
        ref = self.ref_of(at if outgoing else lax.rem(at + 4 - step, 4))
        sem = (self.level, step - 1)
        return remote(ref, ref, self.sems[0].at[sem], self.sems[1].at[sem], self.place.line(self.axis, step))

    def start(self):
        for step in (1, 2, 3):
            self.copy(step, True).start()

    def arrive(self):
        for step in (1, 2, 3):
            self.copy(step, False).wait_recv()

    def drain(self):
        for step in (1, 2, 3):
            self.copy(step, True).wait_send()


def kernel(
    x_ref, g_ref, gain_ref, small_ref, gate_w, cand_w, out_w,
    layer_ref, grad_ref, state_grad_ref, bias_grad_ref,
    weights, smalls, pair, x_p, g_p, normed, inverse, retain, update, cand, back, factor,
    states, gate_g, cand_g, seg_keep, seg_end, seg_carry, enter, leave, sums, vectors, bias_acc,
    red0, red_in, red_x, red_y,
    own_sem, send_sem, recv_sem, sib_send, sib_recv, small_send, small_recv, sum_send, sum_recv,
    red_send, red_recv, last_send, last_recv,
):
    place = Place()
    core = place.core
    z, x, y = place.at["z"], place.at["x"], place.at["y"]
    shards = (out_w, gate_w, cand_w)
    own = []
    for w in range(3):
        for half in range(2):
            copy = pltpu.make_async_copy(
                shards[w].at[pl.ds(16 * half, 16), :], weights.at[w, z, x, y, half], own_sem.at[w, half]
            )
            copy.start()
            own.append(copy)
    lane = lax.broadcasted_iota(jnp.int32, (2, 128), 1)
    smalls[z, x, y] = jnp.where(lane // 32 == y, small_ref[...], 0.0)

    barrier = pltpu.get_barrier_semaphore()
    peers = [place.line(a, d) for a in "xy" for d in (1, 2, 3)]
    peers += [place.column(dz, dc) for dz in range(8) for dc in range(2) if dz or dc]
    for peer in peers:
        pl.semaphore_signal(barrier, inc=1, device_id=peer, device_id_type=MESH)
    pl.semaphore_wait(barrier, len(peers))
    for copy in own:
        copy.wait()

    gather = Weights(place, weights, send_sem, recv_sem, sib_send, sib_recv)
    small_lines = [
        LineExchange(place, "y", lambda v: smalls.at[z, x, v], small_send, small_recv, 0),
        LineExchange(place, "x", lambda v: smalls.at[z, v], small_send, small_recv, 1),
        LineExchange(place, "z", lambda v: smalls.at[v], small_send, small_recv, 2),
    ]

    def blocks(body):
        @pl.loop(0, WIDTH // BLOCK)
        def _(n):
            body(pl.ds(pl.multiple_of(n * BLOCK, BLOCK), BLOCK), n)

    row = lax.broadcasted_iota(jnp.int32, (TOKENS, TOKENS), 0)
    column = lax.broadcasted_iota(jnp.int32, (TOKENS, TOKENS), 1)

    gather.open(0, 0)
    small_lines[0].start()
    gather.near(0, 0)
    small_lines[0].arrive()
    small_lines[1].start()
    gather.far(0, 0)
    gather.open(1, 0)
    permute = jnp.where(column == lax.rem(row, 8) * STEPS + row // 8, 1.0, 0.0).astype(BF16)

    inverse[...] = jnp.zeros_like(inverse)

    def prepare(cols, n):
        rows = jnp.dot(permute, x_ref[:, cols], preferred_element_type=F32)
        x_p[:, cols] = rows.astype(BF16)
        inverse[...] += jnp.sum(rows * rows, axis=1, keepdims=True)
        g_p[:, cols] = jnp.dot(permute, g_ref[:, cols], preferred_element_type=F32).astype(BF16)

    blocks(prepare)
    gather.near(1, 0)
    small_lines[1].arrive()
    small_lines[2].start()
    gather.far(1, 0)

    gather.open(2, 0)
    gather.open(2, 1)
    inverse[...] = lax.rsqrt(inverse[...] * (1.0 / WIDTH) + EPSILON)

    def normalise(cols, n):
        normed[:, cols] = (x_p[:, cols].astype(F32) * inverse[...] * gain_ref[:, cols]).astype(BF16)

    blocks(normalise)
    small_lines[2].arrive()
    for i in range(4):
        for j in range(4):
            pair[:, pl.ds((4 * i + j) * 128, 128)] = (
                smalls[i, j, 0] + smalls[i, j, 1] + smalls[i, j, 2] + smalls[i, j, 3]
            )
    for w in range(3):
        for phase in range(2):
            gather.shared(w, phase, 0)

    def forward_scan(lo):
        lanes = pl.ds(lo, LANES)
        bias = pair[0:1, lanes]

        def step(i, carry):
            reach, state = carry
            rows = pl.ds(pl.multiple_of(i * 8, 8), 8)
            gate = retain[rows, lanes] + bias
            fade = jnp.exp(-jnp.abs(gate))
            high = 1.0 / (1.0 + fade)
            low = fade * high
            up = gate >= 0.0
            u = jnp.where(up, high, low)
            r = jnp.where(up, low, high)
            update[rows, lanes] = u
            retain[rows, lanes] = r
            return reach * r, r * state + u * cand[rows, lanes]

        start = (jnp.ones((8, LANES), F32), jnp.zeros((8, LANES), F32))
        reach, state = lax.fori_loop(0, STEPS, step, start, unroll=4)
        seg_keep[:, lanes] = reach
        seg_end[:, lanes] = state

    def chunk(q):
        gather.shared(1, 2, q)
        gather.shared(2, 2, q)

        @pl.loop(0, SPAN // BLOCK)
        def _(n):
            cols = pl.ds(pl.multiple_of(q * SPAN + n * BLOCK, BLOCK), BLOCK)
            for w, dst in ((1, retain), (2, cand)):
                block = weights[w, :, :, :, :, :, cols].reshape(WIDTH, BLOCK)
                dst[:, cols] = jnp.dot(normed[...], block, preferred_element_type=F32).astype(BF16).astype(F32)

        forward_scan(q * SPAN)
        gather.shared(0, 2, q)

        @pl.loop(0, 2)
        def _(n):
            block = weights[0, pl.ds(2 * n, 2), q].reshape(BLOCK, WIDTH)
            rows = lax.dot_general(g_p[...], block, NT, preferred_element_type=F32).astype(BF16).astype(F32)
            lo = pl.multiple_of(n * 1024 + q * 128, 128)
            back[:, pl.ds(lo, 128)] = rows[:, :128]
            back[:, pl.ds(pl.multiple_of(lo + 512, 128), 128)] = rows[:, 128:]

    for q in range(CHUNKS + 2):
        if q < CHUNKS:
            gather.near(2, q)
            if q + 2 < CHUNKS:
                gather.open(2, q + 2)
        if 1 <= q <= CHUNKS:
            gather.far(2, q - 1)
        if q >= 2:
            chunk(q - 2)

    for lo in range(0, WIDTH, LANES):
        lanes = pl.ds(lo, LANES)

        def step(i, carry):
            rows = pl.ds(pl.multiple_of((STEPS - 1 - i) * 8, 8), 8)
            return retain[rows, lanes] * (back[rows, lanes] + carry)

        seg_carry[:, lanes] = lax.fori_loop(0, STEPS, step, jnp.zeros((8, LANES), F32), unroll=4)

    keep, end, carry = seg_keep[0:1], seg_end[0:1], seg_carry[7:8]
    for k in range(1, 8):
        end = seg_keep[k : k + 1] * end + seg_end[k : k + 1]
        keep = keep * seg_keep[k : k + 1]
        carry = seg_carry[7 - k : 8 - k] + seg_keep[7 - k : 8 - k] * carry
    total = (keep, end, carry)
    lines = []
    for level, axis in enumerate("yxz"):
        at = place.at[axis]
        for k in range(3):
            sums[level, at, k : k + 1, :] = total[k]
        line = LineExchange(place, axis, lambda v, level=level: sums.at[level, v], sum_send, sum_recv, level)
        line.start()
        line.arrive()
        lines.append(line)
        keeps = [sums[level, m, 0:1, :] for m in range(4)]
        ends = [sums[level, m, 1:2, :] for m in range(4)]
        carries = [sums[level, m, 2:3, :] for m in range(4)]
        one, zero = jnp.ones((1, WIDTH), F32), jnp.zeros((1, WIDTH), F32)
        before, arrived, after, returned = one, zero, one, zero
        for m in range(3):
            take = m < at
            arrived = jnp.where(take, keeps[m] * arrived + ends[m], arrived)
            before = jnp.where(take, keeps[m] * before, before)
        for m in (3, 2, 1):
            take = m > at
            returned = jnp.where(take, carries[m] + keeps[m] * returned, returned)
            after = jnp.where(take, keeps[m] * after, after)
        for k, value in enumerate((before, arrived, after, returned)):
            vectors[4 * level + k] = value
        keep, end, carry = keeps[0], ends[0], carries[3]
        for m in range(1, 4):
            end = keeps[m] * end + ends[m]
            keep = keep * keeps[m]
            carry = carries[3 - m] + keeps[3 - m] * carry
        total = (keep, end, carry)
    vectors[12] = total[2]
    entering, leaving = pair[1:2, :], jnp.zeros((1, WIDTH), F32)
    for level in (2, 1, 0):
        entering = vectors[4 * level] * entering + vectors[4 * level + 1]
        leaving = vectors[4 * level + 2] * leaving + vectors[4 * level + 3]
    for k in range(8):
        enter[k : k + 1, :] = entering
        leave[7 - k : 8 - k, :] = leaving
        if k < 7:
            entering = seg_keep[k : k + 1] * entering + seg_end[k : k + 1]
            leaving = seg_keep[7 - k : 8 - k] * leaving + seg_carry[7 - k : 8 - k]
    own_lanes = pl.ds(pl.multiple_of((z * 4 + x) * 128, 128), 128)
    turn = lax.rem(128 - 32 * y, 128)
    state_grad_ref[...] = pltpu.roll(vectors[12, :, own_lanes], turn, 1)[:, :32]

    for lo in range(0, WIDTH, LANES):
        lanes = pl.ds(lo, LANES)

        def step(i, state):
            halves = []
            for k in range(2):
                rows = pl.ds(pl.multiple_of(i * 16 + k * 8, 8), 8)
                r, u, c = retain[rows, lanes], update[rows, lanes], cand[rows, lanes]
                factor[rows, lanes] = (c - state) * u * r
                state = r * state + u * c
                halves.append(state)
            states[pl.ds(pl.multiple_of(i * 16, 16), 16), lanes] = jnp.concatenate(halves, axis=0).astype(BF16)
            return state

        lax.fori_loop(0, STEPS // 2, step, enter[:, lanes], unroll=2)

    for lo in range(0, WIDTH, LANES):
        lanes = pl.ds(lo, LANES)

        def step(i, carry):
            coming, total_bias = carry
            gates, cands = [None, None], [None, None]
            for k in (1, 0):
                rows = pl.ds(pl.multiple_of((STEPS // 2 - 1 - i) * 16 + k * 8, 8), 8)
                carried = back[rows, lanes] + coming
                gates[k] = carried * factor[rows, lanes]
                cands[k] = carried * update[rows, lanes]
                coming = retain[rows, lanes] * carried
                total_bias = total_bias + gates[k]
            rows = pl.ds(pl.multiple_of((STEPS // 2 - 1 - i) * 16, 16), 16)
            gate_g[rows, lanes] = jnp.concatenate(gates, axis=0).astype(BF16)
            cand_g[rows, lanes] = jnp.concatenate(cands, axis=0).astype(BF16)
            return coming, total_bias

        start = (leave[:, lanes], jnp.zeros((8, LANES), F32))
        _, total_bias = lax.fori_loop(0, STEPS // 2, step, start, unroll=2)
        bias_acc[:, lanes] = jnp.sum(total_bias, axis=0, keepdims=True)

    for i in range(4):
        for j in range(4):
            red0[i, j : j + 1, :] = bias_acc[:, pl.ds((4 * i + j) * 128, 128)]

    def reduce_copy(dz, dc):
        k = dz * 2 + dc
        return remote(
            red0.at[lax.rem(z + dz, 4)], red_in.at[k], red_send.at[k], red_recv.at[k], place.column(dz, dc)
        )

    column_peers = [(dz, dc) for dz in range(8) for dc in range(2) if dz or dc]
    for dz, dc in column_peers:
        reduce_copy(dz, dc).start()

    restore = jnp.where(row == lax.rem(column, 8) * STEPS + column // 8, 1.0, 0.0).astype(BF16)

    def layer(cols, n):
        block = weights[0, :, :, :, :, :, cols].reshape(WIDTH, BLOCK)
        rows = x_p[:, cols].astype(F32) + jnp.dot(states[...], block, preferred_element_type=F32)
        layer_ref[:, cols] = jnp.dot(restore, rows.astype(BF16), preferred_element_type=F32).astype(BF16)

    blocks(layer)

    for dz, dc in column_peers:
        reduce_copy(dz, dc).wait_recv()
    part = red0[z]
    for dz, dc in column_peers:
        part = part + red_in[dz * 2 + dc]
    for j in range(4):
        red_x[0, j] = part[j : j + 1, :]

    def copy_x(step):
        return remote(
            red_x.at[0, lax.rem(x + step, 4)], red_x.at[step, 0], last_send.at[0, step - 1],
            last_recv.at[0, step - 1], place.line("x", step),
        )

    for step in (1, 2, 3):
        copy_x(step).start()

    inverse_rows = inverse[...]
    row_sum = jnp.zeros((TOKENS, 1), F32)

    def unit_block(n, row_sum):
        cols = pl.ds(pl.multiple_of(n * BLOCK, BLOCK), BLOCK)
        which = pl.ds(2 * lax.rem(n, 2), 2)
        gate_block = weights[1, n // 2, which].reshape(BLOCK, WIDTH)
        cand_block = weights[2, n // 2, which].reshape(BLOCK, WIDTH)
        rows = lax.dot_general(gate_g[...], gate_block, NT, preferred_element_type=F32)
        rows = rows + lax.dot_general(cand_g[...], cand_block, NT, preferred_element_type=F32)
        rows = rows * gain_ref[:, cols]
        factor[:, cols] = rows
        unit = x_p[:, cols].astype(F32) * inverse_rows
        return row_sum + jnp.sum(rows * unit, axis=1, keepdims=True)

    row_sum = lax.fori_loop(0, 4, unit_block, row_sum)
    for step in (1, 2, 3):
        copy_x(step).wait_recv()
    red_y[y] = red_x[0, x] + red_x[1, 0] + red_x[2, 0] + red_x[3, 0]
    last_line = LineExchange(place, "y", lambda v: red_y.at[v], last_send, last_recv, 1)
    last_line.start()
    row_sum = lax.fori_loop(4, 8, unit_block, row_sum)
    last_line.arrive()
    bias_total = red_y[0] + red_y[1] + red_y[2] + red_y[3]
    bias_grad_ref[...] = pltpu.roll(bias_total, turn, 1)[:, :32]
    mean = row_sum * (1.0 / WIDTH)

    def finish(cols, n):
        unit = x_p[:, cols].astype(F32) * inverse_rows
        rows = g_p[:, cols].astype(F32) + inverse_rows * (factor[:, cols] - unit * mean)
        grad_ref[:, cols] = jnp.dot(restore, rows.astype(BF16), preferred_element_type=F32).astype(BF16)

    blocks(finish)

    for phase in range(3):
        for q in range(CHUNKS if phase == 2 else 1):
            gather.drain(phase, q)
    for line in small_lines + lines + [last_line]:
        line.drain()
    for dz, dc in column_peers:
        reduce_copy(dz, dc).wait_send()
    for step in (1, 2, 3):
        copy_x(step).wait_send()


def on_device(inputs, output_grad, norm_gain, gate_bias, state_in, w_gate, w_cand, w_out):
    small = jnp.stack([jnp.tile(gate_bias, 4), jnp.tile(state_in[0], 4)])
    whole = lambda rows, dtype: pltpu.VMEM((rows, WIDTH), dtype)
    dma = pltpu.SemaphoreType.DMA
    layer, grad, state_grad, bias_grad = pl.pallas_call(
        kernel,
        out_shape=(
            jax.ShapeDtypeStruct((TOKENS, WIDTH), BF16),
            jax.ShapeDtypeStruct((TOKENS, WIDTH), BF16),
            jax.ShapeDtypeStruct((1, 32), F32),
            jax.ShapeDtypeStruct((1, 32), F32),
        ),
        in_specs=[pl.BlockSpec(memory_space=pltpu.VMEM)] * 7,
        out_specs=[pl.BlockSpec(memory_space=pltpu.VMEM)] * 4,
        scratch_shapes=[
            pltpu.VMEM((3, 4, 4, 4, 2, 16, WIDTH), BF16),
            pltpu.VMEM((4, 4, 4, 2, 128), F32),
            whole(2, F32),
            whole(TOKENS, BF16), whole(TOKENS, BF16), whole(TOKENS, BF16),
            pltpu.VMEM((TOKENS, 1), F32),
            whole(TOKENS, F32), whole(TOKENS, F32), whole(TOKENS, F32), whole(TOKENS, F32), whole(TOKENS, F32),
            whole(TOKENS, BF16), whole(TOKENS, BF16), whole(TOKENS, BF16),
            whole(8, F32), whole(8, F32), whole(8, F32), whole(8, F32), whole(8, F32),
            pltpu.VMEM((3, 4, 4, WIDTH), F32),
            pltpu.VMEM((13, 1, WIDTH), F32),
            whole(1, F32),
            pltpu.VMEM((4, 4, 128), F32),
            pltpu.VMEM((16, 4, 128), F32),
            pltpu.VMEM((4, 4, 1, 128), F32),
            pltpu.VMEM((4, 1, 128), F32),
            dma((3, 2)),
            dma((3, 3, 4, CHUNKS)), dma((3, 3, 4, CHUNKS)), dma((3, 3, 4, CHUNKS)), dma((3, 3, 4, CHUNKS)),
            dma((3, 3)), dma((3, 3)), dma((3, 3)), dma((3, 3)),
            dma((16,)), dma((16,)), dma((2, 3)), dma((2, 3)),
        ],
        compiler_params=pltpu.CompilerParams(
            collective_id=0, has_side_effects=True, vmem_limit_bytes=62 * 1024 * 1024
        ),
        name="mixer",
    )(inputs[0], output_grad[0], norm_gain[None], small, w_gate, w_cand, w_out)
    return (layer[None], grad[None], state_grad, bias_grad[0])


def solution(mesh):
    return jax.shard_map(
        on_device,
        mesh=mesh,
        in_specs=(
            P("batch", "seq", None),
            P("batch", "seq", None),
            P(),
            P("seq"),
            P("batch", "seq"),
            P("seq", None),
            P("seq", None),
            P("seq", None),
        ),
        out_specs=(P("batch", "seq", None), P("batch", "seq", None), P("batch", "seq"), P("seq")),
        check_vma=False,
    )
```

```python
import jax
import jax.numpy as jnp
from jax import lax
from jax.sharding import PartitionSpec as P
from jax.experimental import pallas as pl
from jax.experimental.pallas import tpu as pltpu

EPSILON = 1e-06
MESH = pl.DeviceIdType.MESH
ORDERS = ("xyz", "yzx", "zxy")
AXIS_DIM = {"z": 0, "x": 1, "y": 2}
CHUNKS = 4
TOKENS = 256
WIDTH = 2048
SPAN = WIDTH // CHUNKS
BLOCK = 512
STEPS = TOKENS // 8
UNROLL = 32
LANES = 512
F32 = jnp.float32
BF16 = jnp.bfloat16
NT = (((1,), (1,)), ((), ()))


class Place:
    def __init__(self):
        seq = lax.axis_index("seq")
        batch = lax.axis_index("batch")
        self.seq, self.batch = seq, batch
        self.at = {"z": seq // 16, "x": lax.rem(seq // 4, 4), "y": lax.rem(seq, 4)}
        self.z_hi = batch // 2
        self.core = lax.rem(batch, 2)

    def device(self, z, x, y, z_hi, core):
        return (z * 16 + x * 4 + y, z_hi * 2 + core)

    def line(self, axis, step):
        at = dict(self.at)
        at[axis] = lax.rem(at[axis] + 4 + step, 4)
        return self.device(at["z"], at["x"], at["y"], self.z_hi, self.core)

    def column(self, step, flip):
        full = lax.rem(self.z_hi * 4 + self.at["z"] + 8 + step, 8)
        core = lax.rem(self.core + flip, 2)
        return self.device(lax.rem(full, 4), self.at["x"], self.at["y"], full // 4, core)

    def ring(self, axis, step):
        return self.column(step, 0) if axis == "z" else self.line(axis, step)

    def sibling(self):
        return self.column(0, 1)


def remote(src, dst, send_sem, recv_sem, device):
    return pltpu.make_async_remote_copy(
        src_ref=src, dst_ref=dst, send_sem=send_sem, recv_sem=recv_sem, device_id=device, device_id_type=MESH
    )


class Weights:
    def __init__(self, place, buffer, send_sem, recv_sem, sib_send, sib_recv):
        self.place, self.buffer = place, buffer
        self.sems, self.sib_sems = (send_sem, recv_sem), (sib_send, sib_recv)

    def slab(self, w, phase, step, which, q, part, prev=None):
        index = [None, None, None]
        for position, axis in enumerate(ORDERS[w]):
            own_at = self.place.at[axis]
            if position == phase - 1 and prev is not None:
                index[AXIS_DIM[axis]] = lax.rem(own_at + 4 + prev, 4)
            elif position < phase:
                index[AXIS_DIM[axis]] = slice(None)
            elif position == phase:
                index[AXIS_DIM[axis]] = lax.rem(own_at + 4 + step, 4)
            else:
                index[AXIS_DIM[axis]] = own_at
        start, width = 0, WIDTH
        if phase == 2 and w == 0:
            index[AXIS_DIM["x"]] = q
        elif phase == 2:
            start, width = q * SPAN, SPAN
        if part is not None:
            width = width // 2
            start = start + part * width
        return self.buffer.at[w, index[0], index[1], index[2], which, :, pl.ds(start, width)]

    def piece(self, w, phase, kind, q, which, outgoing):
        right = kind % 2 == 0
        if kind < 2:
            step, part = (0 if outgoing else (-1 if right else 1)), None
        else:
            step, part = ((-1 if right else 1) if outgoing else 2), kind - 2
        return self.slab(w, phase, step, which, q, part)

    def copy(self, ref, w, phase, kind, q):
        device = self.place.ring(ORDERS[w][phase], 1 if kind % 2 == 0 else -1)
        at = (w, phase, kind, q)
        return remote(ref, ref, self.sems[0].at[at], self.sems[1].at[at], device)

    def hop(self, w, phase, kind, q, outgoing):
        return self.copy(self.piece(w, phase, kind, q, self.place.core, outgoing), w, phase, kind, q)

    def share(self, w, phase, kind, q, mine):
        ref = self.piece(w, phase, kind, q, self.place.core if mine else 1 - self.place.core, False)
        at = (w, phase, kind, q)
        return remote(ref, ref, self.sib_sems[0].at[at], self.sib_sems[1].at[at], self.place.sibling())

    def part(self, w, phase, q, prev):
        for kind in (0, 1):
            self.copy(self.slab(w, phase, 0, self.place.core, q, None, prev), w, phase, kind, q).start()

    def open(self):
        for w in range(3):
            for kind in (0, 1):
                self.hop(w, 0, kind, 0, True).start()
        for w in range(3):
            self.part(w, 1, 0, 0)

    def near(self, phase, q):
        ahead = {0: (0,), 1: (0, 1), 2: ()}[phase]
        for w in range(3):
            for kind in (0, 1):
                self.hop(w, phase, kind, q, False).wait_recv()
                self.hop(w, phase, kind + 2, q, True).start()
                self.share(w, phase, kind, q, True).start()
                for later in ahead:
                    self.part(w, phase + 1, later, 1 if kind else -1)

    def far(self, phase, q):
        for w in range(3):
            for kind in (2, 3):
                self.hop(w, phase, kind, q, False).wait_recv()
                self.share(w, phase, kind, q, True).start()
            if phase == 0:
                self.part(w, 1, 0, 2)
            if phase == 1:
                for later in (0, 1):
                    self.part(w, 2, later, 2)
        if phase == 0:
            for later in range(CHUNKS):
                for w in range(3):
                    self.part(w, 2, later, 0)

    def rest(self, q, prevs):
        for w in range(3):
            for prev in prevs:
                self.part(w, 2, q, prev)

    def shared(self, w, phase, q):
        for kind in range(4):
            self.share(w, phase, kind, q, False).wait_recv()

    def drain(self, phase, q):
        for w in range(3):
            for kind in range(4):
                self.hop(w, phase, kind, q, True).wait_send()
                self.share(w, phase, kind, q, True).wait_send()


class LineExchange:
    def __init__(self, place, axis, ref_of, send_sem, recv_sem, level):
        self.place, self.axis, self.ref_of = place, axis, ref_of
        self.sems, self.level = (send_sem, recv_sem), level

    def copy(self, step, outgoing):
        at = self.place.at[self.axis]
        ref = self.ref_of(at if outgoing else lax.rem(at + 4 - step, 4))
        sem = (self.level, step - 1)
        return remote(ref, ref, self.sems[0].at[sem], self.sems[1].at[sem], self.place.line(self.axis, step))

    def start(self):
        for step in (1, 2, 3):
            self.copy(step, True).start()

    def arrive(self):
        for step in (1, 2, 3):
            self.copy(step, False).wait_recv()

    def drain(self):
        for step in (1, 2, 3):
            self.copy(step, True).wait_send()


def kernel(
    x_hbm, g_hbm, gain_ref, bias_ref, state_ref, gate_w, cand_w, out_w,
    layer_ref, grad_ref, state_grad_ref, bias_grad_ref,
    weights, smalls, pair, x_in, g_in, x_p, g_p, normed, inverse, retain, update, cand, back, factor,
    states, gate_g, cand_g, layer_acc, grad_acc, seg_keep, seg_end, seg_carry, enter, leave, sums, vectors, bias_acc,
    red0, red_in, red_x, red_y,
    own_sem, in_sem, send_sem, recv_sem, sib_send, sib_recv, small_send, small_recv, sum_send, sum_recv,
    red_send, red_recv, last_send, last_recv,
):
    place = Place()
    z, x, y = place.at["z"], place.at["x"], place.at["y"]
    barrier = pltpu.get_barrier_semaphore()
    column_peers = [(dz, dc) for dz in range(8) for dc in range(2) if dz or dc]
    peers = [place.line(a, d) for a in "xy" for d in (1, 2, 3)]
    peers += [place.column(dz, dc) for dz, dc in column_peers]
    for peer in peers:
        pl.semaphore_signal(barrier, inc=1, device_id=peer, device_id_type=MESH)

    read_x = pltpu.make_async_copy(x_hbm, x_in, in_sem.at[0])
    read_g = pltpu.make_async_copy(g_hbm, g_in, in_sem.at[1])
    own = [pltpu.make_async_copy(w, weights.at[k, z, x, y], own_sem.at[k]) for k, w in enumerate((out_w, gate_w, cand_w))]
    read_x.start()
    own[0].start()
    for k, w in ((1, gate_w), (2, cand_w)):
        for q in range(4):
            for i in range(4):
                pltpu.make_async_copy(
                    w.at[:, :, pl.ds((i * 4 + q) * 128, 128)],
                    weights.at[k, z, x, y, :, :, pl.ds((q * 4 + i) * 128, 128)],
                    own_sem.at[k],
                ).start()
    read_g.start()
    lane = lax.broadcasted_iota(jnp.int32, (2, 128), 1)
    small = [jnp.concatenate([ref[...]] * 4, axis=1) for ref in (bias_ref, state_ref)]
    smalls[z, x, y] = jnp.where(lane // 32 == y, jnp.concatenate(small, axis=0), 0.0)

    gather = Weights(place, weights, send_sem, recv_sem, sib_send, sib_recv)
    small_lines = [
        LineExchange(place, "y", lambda v: smalls.at[z, x, v], small_send, small_recv, 0),
        LineExchange(place, "x", lambda v: smalls.at[z, v], small_send, small_recv, 1),
        LineExchange(place, "z", lambda v: smalls.at[v], small_send, small_recv, 2),
    ]

    def blocks(body):
        @pl.loop(0, WIDTH // BLOCK)
        def _(n):
            body(pl.ds(pl.multiple_of(n * BLOCK, BLOCK), BLOCK), n)

    row = lax.broadcasted_iota(jnp.int32, (TOKENS, TOKENS), 0)
    column = lax.broadcasted_iota(jnp.int32, (TOKENS, TOKENS), 1)
    permute = jnp.where(column == lax.rem(row, 8) * STEPS + row // 8, 1.0, 0.0).astype(BF16)
    inverse[...] = jnp.zeros_like(inverse)

    def prepare(cols, n):
        rows = jnp.dot(permute, x_in[:, cols], preferred_element_type=F32)
        x_p[:, cols] = rows.astype(BF16)
        inverse[...] += jnp.sum(rows * rows, axis=1, keepdims=True)

    def prepare_grads(cols, n):
        g_p[:, cols] = jnp.dot(permute, g_in[:, cols], preferred_element_type=F32).astype(BF16)

    def normalise(cols, n):
        normed[:, cols] = (x_p[:, cols].astype(F32) * inverse[...] * gain_ref[:, cols]).astype(BF16)

    read_x.wait()
    blocks(prepare)
    inverse[...] = lax.rsqrt(inverse[...] * (1.0 / WIDTH) + EPSILON)
    for copy in own:
        copy.wait()
    pl.semaphore_wait(barrier, len(peers))

    small_lines[0].start()
    gather.open()
    read_g.wait()
    blocks(prepare_grads)
    small_lines[0].arrive()
    small_lines[1].start()
    gather.near(0, 0)
    gather.far(0, 0)
    blocks(normalise)
    small_lines[1].arrive()
    small_lines[2].start()
    gather.near(1, 0)
    gather.far(1, 0)

    def gather_pair():
        small_lines[2].arrive()
        for i in range(4):
            for j in range(4):
                pair[:, pl.ds((4 * j + i) * 128, 128)] = (
                    smalls[i, j, 0] + smalls[i, j, 1] + smalls[i, j, 2] + smalls[i, j, 3]
                )

    def stage_gates(q):
        gather.shared(1, 2, q)
        gather.shared(2, 2, q)
        lanes = pl.ds(q * SPAN, SPAN)
        for w, dst in ((1, retain), (2, cand)):
            block = weights[w, :, :, :, :, :, lanes].reshape(WIDTH, SPAN)
            dst[:, lanes] = jnp.dot(normed[...], block, preferred_element_type=F32).astype(BF16).astype(F32)

    def forward_scan(q):
        lanes = pl.ds(q * SPAN, SPAN)
        bias = pair[0:1, lanes]

        def step(i, carry):
            reach, state = carry
            rows = pl.ds(pl.multiple_of(i * 8, 8), 8)
            gate = retain[rows, lanes] + bias
            fade = jnp.exp(-jnp.abs(gate))
            high = 1.0 / (1.0 + fade)
            low = fade * high
            up = gate >= 0.0
            u = jnp.where(up, high, low)
            r = jnp.where(up, low, high)
            update[rows, lanes] = u
            retain[rows, lanes] = r
            return reach * r, r * state + u * cand[rows, lanes]

        start = (jnp.ones((8, SPAN), F32), jnp.zeros((8, SPAN), F32))
        reach, state = lax.fori_loop(0, STEPS, step, start, unroll=UNROLL)
        seg_keep[:, lanes] = reach
        seg_end[:, lanes] = state

    def stage_back(q):
        gather.shared(0, 2, q)
        block = weights[0, :, q].reshape(SPAN, WIDTH)
        rows = lax.dot_general(g_p[...], block, NT, preferred_element_type=F32)
        back[:, pl.ds(q * SPAN, SPAN)] = rows.astype(BF16).astype(F32)

    def backward_scan(q):
        lanes = pl.ds(q * SPAN, SPAN)

        def step(i, carry):
            rows = pl.ds(pl.multiple_of((STEPS - 1 - i) * 8, 8), 8)
            return retain[rows, lanes] * (back[rows, lanes] + carry)

        seg_carry[:, lanes] = lax.fori_loop(0, STEPS, step, jnp.zeros((8, SPAN), F32), unroll=UNROLL)

    lines = [
        [
            LineExchange(
                place, axis, lambda v, level=level, q=q: sums.at[level, q, v], sum_send, sum_recv, level * CHUNKS + q
            )
            for q in range(CHUNKS)
        ]
        for level, axis in enumerate("yxz")
    ]

    def publish(level, q, total):
        at = place.at["yxz"[level]]
        for k in range(3):
            sums[level, q, at, k : k + 1, :] = total[k]
        lines[level][q].start()

    def summarise(q):
        lanes = pl.ds(q * SPAN, SPAN)
        keeps, ends, carries = seg_keep[:, lanes], seg_end[:, lanes], seg_carry[:, lanes]
        keep, end, carry = keeps[0:1], ends[0:1], carries[7:8]
        for k in range(1, 8):
            end = keeps[k : k + 1] * end + ends[k : k + 1]
            keep = keep * keeps[k : k + 1]
            carry = carries[7 - k : 8 - k] + keeps[7 - k : 8 - k] * carry
        publish(0, q, (keep, end, carry))

    def compose(level, q):
        at = place.at["yxz"[level]]
        lines[level][q].arrive()
        keeps = [sums[level, q, m, 0:1, :] for m in range(4)]
        ends = [sums[level, q, m, 1:2, :] for m in range(4)]
        carries = [sums[level, q, m, 2:3, :] for m in range(4)]
        keep, end, carry = keeps[0], ends[0], carries[3]
        for m in range(1, 4):
            end = keeps[m] * end + ends[m]
            keep = keep * keeps[m]
            carry = carries[3 - m] + keeps[3 - m] * carry
        if level < 2:
            publish(level + 1, q, (keep, end, carry))
        else:
            vectors[q, 12] = carry
        one, zero = jnp.ones((1, SPAN), F32), jnp.zeros((1, SPAN), F32)
        before, arrived, after, returned = one, zero, one, zero
        for m in range(3):
            take = m < at
            arrived = jnp.where(take, keeps[m] * arrived + ends[m], arrived)
            before = jnp.where(take, keeps[m] * before, before)
        for m in (3, 2, 1):
            take = m > at
            returned = jnp.where(take, carries[m] + keeps[m] * returned, returned)
            after = jnp.where(take, keeps[m] * after, after)
        for k, value in enumerate((before, arrived, after, returned)):
            vectors[q, 4 * level + k] = value

    def settle(q):
        lanes = pl.ds(q * SPAN, SPAN)
        entering, leaving = pair[1:2, lanes], jnp.zeros((1, SPAN), F32)
        for level in (2, 1, 0):
            entering = vectors[q, 4 * level] * entering + vectors[q, 4 * level + 1]
            leaving = vectors[q, 4 * level + 2] * leaving + vectors[q, 4 * level + 3]
        keeps, ends, carries = seg_keep[:, lanes], seg_end[:, lanes], seg_carry[:, lanes]
        for k in range(8):
            enter[k : k + 1, lanes] = entering
            leave[7 - k : 8 - k, lanes] = leaving
            if k < 7:
                entering = keeps[k : k + 1] * entering + ends[k : k + 1]
                leaving = keeps[7 - k : 8 - k] * leaving + carries[7 - k : 8 - k]

    def gradients(q):
        lanes = pl.ds(q * SPAN, SPAN)

        def ahead(i, state):
            halves = []
            for k in range(2):
                rows = pl.ds(pl.multiple_of(i * 16 + k * 8, 8), 8)
                r, u, c = retain[rows, lanes], update[rows, lanes], cand[rows, lanes]
                factor[rows, lanes] = (c - state) * u * r
                state = r * state + u * c
                halves.append(state)
            states[pl.ds(pl.multiple_of(i * 16, 16), 16), lanes] = jnp.concatenate(halves, axis=0).astype(BF16)
            return state

        lax.fori_loop(0, STEPS // 2, ahead, enter[:, lanes], unroll=2)

        def astern(i, carry):
            coming, total_bias = carry
            gates, cands = [None, None], [None, None]
            for k in (1, 0):
                rows = pl.ds(pl.multiple_of((STEPS // 2 - 1 - i) * 16 + k * 8, 8), 8)
                carried = back[rows, lanes] + coming
                gates[k] = carried * factor[rows, lanes]
                cands[k] = carried * update[rows, lanes]
                coming = retain[rows, lanes] * carried
                total_bias = total_bias + gates[k]
            rows = pl.ds(pl.multiple_of((STEPS // 2 - 1 - i) * 16, 16), 16)
            gate_g[rows, lanes] = jnp.concatenate(gates, axis=0).astype(BF16)
            cand_g[rows, lanes] = jnp.concatenate(cands, axis=0).astype(BF16)
            return coming, total_bias

        start = (leave[:, lanes], jnp.zeros((8, SPAN), F32))
        _, total_bias = lax.fori_loop(0, STEPS // 2, astern, start, unroll=2)
        bias_acc[:, lanes] = jnp.sum(total_bias, axis=0, keepdims=True)
        for i in range(4):
            red0[i, q : q + 1, :] = bias_acc[:, pl.ds((4 * q + i) * 128, 128)]

    def layer_part(q, cols):
        block = weights[0, :, q, :, :, :, cols].reshape(SPAN, BLOCK)
        return jnp.dot(states[:, pl.ds(q * SPAN, SPAN)], block, preferred_element_type=F32)

    def grad_part(q, n):
        lanes = pl.ds(q * SPAN, SPAN)
        rows = None
        for w, value in ((1, gate_g), (2, cand_g)):
            block = weights[w, n, :, :, :, :, lanes].reshape(BLOCK, SPAN)
            term = lax.dot_general(value[:, lanes], block, NT, preferred_element_type=F32)
            rows = term if rows is None else rows + term
        return rows

    def accumulate_layer(q):
        def body(cols, n):
            layer_acc[:, cols] = layer_part(q, cols) + (layer_acc[:, cols] if q else x_p[:, cols].astype(F32))

        blocks(body)

    def accumulate_grad(q):
        def body(cols, n):
            grad_acc[:, cols] = grad_part(q, n) + (grad_acc[:, cols] if q else 0.0)

        blocks(body)

    def poll(q):
        if q == 1:
            for w in range(3):
                for phase in range(2):
                    gather.shared(w, phase, 0)
        if 0 <= q < CHUNKS:
            gather.near(2, q)
            if q + 1 < CHUNKS and q:
                gather.rest(q + 1, (1, 2))
            if q + 2 < CHUNKS:
                gather.rest(q + 2, (-1,))
        if 1 <= q <= CHUNKS:
            gather.far(2, q - 1)

    last = CHUNKS - 1
    poll(0)
    for t in range(CHUNKS + 3):
        if t < CHUNKS:
            poll(t + 1)
            stage_gates(t)
            if t == 0:
                gather_pair()
            forward_scan(t)
            stage_back(t)
            backward_scan(t)
            summarise(t)
        for level in range(3):
            if 0 <= t - 1 - level < CHUNKS:
                compose(level, t - 1 - level)
        if t >= 3:
            settle(t - 3)
            gradients(t - 3)
            if t - 3 < last - 1:
                accumulate_layer(t - 3)
                accumulate_grad(t - 3)

    def reduce_copy(dz, dc):
        k = dz * 2 + dc
        return remote(
            red0.at[lax.rem(z + dz, 4)], red_in.at[k], red_send.at[k], red_recv.at[k], place.column(dz, dc)
        )

    for dz, dc in column_peers:
        reduce_copy(dz, dc).start()
    accumulate_layer(last - 1)
    accumulate_grad(last - 1)

    own_lanes = pl.ds(pl.multiple_of(z * 128, 128), 128)
    turn = lax.rem(128 - 32 * y, 128)
    state_grad_ref[...] = pltpu.roll(vectors[x, 12, :, own_lanes], turn, 1)[:, :32]

    inverse_rows = inverse[...]

    def unit_block(n, row_sum):
        cols = pl.ds(pl.multiple_of(n * BLOCK, BLOCK), BLOCK)
        rows = (grad_part(last, n) + grad_acc[:, cols]) * gain_ref[:, cols]
        grad_acc[:, cols] = rows
        unit = x_p[:, cols].astype(F32) * inverse_rows
        return row_sum + jnp.sum(rows * unit, axis=1, keepdims=True)

    row_sum = lax.fori_loop(0, WIDTH // BLOCK, unit_block, jnp.zeros((TOKENS, 1), F32))
    mean = row_sum * (1.0 / WIDTH)

    for dz, dc in column_peers:
        reduce_copy(dz, dc).wait_recv()
    part = red0[z]
    for dz, dc in column_peers:
        part = part + red_in[dz * 2 + dc]
    for j in range(4):
        red_x[0, j] = part[j : j + 1, :]

    def copy_x(step):
        return remote(
            red_x.at[0, lax.rem(x + step, 4)], red_x.at[step, 0], last_send.at[0, step - 1],
            last_recv.at[0, step - 1], place.line("x", step),
        )

    for step in (1, 2, 3):
        copy_x(step).start()

    def finish_layer(cols, n):
        rows = layer_part(last, cols) + layer_acc[:, cols]
        layer_ref[:, cols] = rows.astype(BF16)

    blocks(finish_layer)

    for step in (1, 2, 3):
        copy_x(step).wait_recv()
    red_y[y] = red_x[0, x] + red_x[1, 0] + red_x[2, 0] + red_x[3, 0]
    last_line = LineExchange(place, "y", lambda v: red_y.at[v], last_send, last_recv, 1)
    last_line.start()

    def finish_grad(cols, n):
        unit = x_p[:, cols].astype(F32) * inverse_rows
        rows = g_p[:, cols].astype(F32) + inverse_rows * (grad_acc[:, cols] - unit * mean)
        grad_ref[:, cols] = rows.astype(BF16)

    blocks(finish_grad)

    for phase in range(3):
        for q in range(CHUNKS if phase == 2 else 1):
            gather.drain(phase, q)
    for line in small_lines + lines[0] + lines[1] + lines[2]:
        line.drain()
    for dz, dc in column_peers:
        reduce_copy(dz, dc).wait_send()
    for step in (1, 2, 3):
        copy_x(step).wait_send()
    last_line.arrive()
    bias_total = red_y[0] + red_y[1] + red_y[2] + red_y[3]
    bias_grad_ref[...] = pltpu.roll(bias_total, turn, 1)[:, :32]
    last_line.drain()


def restore_kernel(layer_ref, grad_ref, small0_ref, small1_ref, layer_out, grad_out, small0_out, small1_out):
    row = lax.broadcasted_iota(jnp.int32, (TOKENS, TOKENS), 0)
    column = lax.broadcasted_iota(jnp.int32, (TOKENS, TOKENS), 1)
    restore = jnp.where(row == lax.rem(column, 8) * STEPS + column // 8, 1.0, 0.0).astype(BF16)
    for source, target in ((layer_ref, layer_out), (grad_ref, grad_out)):
        target[...] = jnp.dot(restore, source[...], preferred_element_type=F32).astype(BF16)
    small0_out[...] = small0_ref[...]
    small1_out[...] = small1_ref[...]


def on_device(inputs, output_grad, norm_gain, gate_bias, state_in, w_gate, w_cand, w_out):
    whole = lambda rows, dtype: pltpu.VMEM((rows, WIDTH), dtype)
    dma = pltpu.SemaphoreType.DMA
    anywhere, vmem = pl.BlockSpec(memory_space=pl.ANY), pl.BlockSpec(memory_space=pltpu.VMEM)
    halves = (2, 16, WIDTH)
    layer, grad, state_grad, bias_grad = pl.pallas_call(
        kernel,
        out_shape=(
            jax.ShapeDtypeStruct((TOKENS, WIDTH), BF16),
            jax.ShapeDtypeStruct((TOKENS, WIDTH), BF16),
            jax.ShapeDtypeStruct((1, 32), F32),
            jax.ShapeDtypeStruct((1, 32), F32),
        ),
        in_specs=[anywhere, anywhere, vmem, vmem, vmem, anywhere, anywhere, anywhere],
        out_specs=[vmem] * 4,
        scratch_shapes=[
            pltpu.VMEM((3, 4, 4, 4, 2, 16, WIDTH), BF16),
            pltpu.VMEM((4, 4, 4, 2, 128), F32),
            whole(2, F32),
            whole(TOKENS, BF16), whole(TOKENS, BF16),
            whole(TOKENS, BF16), whole(TOKENS, BF16), whole(TOKENS, BF16),
            pltpu.VMEM((TOKENS, 1), F32),
            whole(TOKENS, F32), whole(TOKENS, F32), whole(TOKENS, F32), whole(TOKENS, F32), whole(TOKENS, F32),
            whole(TOKENS, BF16), whole(TOKENS, BF16), whole(TOKENS, BF16),
            whole(TOKENS, F32), whole(TOKENS, F32),
            whole(8, F32), whole(8, F32), whole(8, F32), whole(8, F32), whole(8, F32),
            pltpu.VMEM((3, CHUNKS, 4, 4, SPAN), F32),
            pltpu.VMEM((CHUNKS, 13, 1, SPAN), F32),
            whole(1, F32),
            pltpu.VMEM((4, 4, 128), F32),
            pltpu.VMEM((16, 4, 128), F32),
            pltpu.VMEM((4, 4, 1, 128), F32),
            pltpu.VMEM((4, 1, 128), F32),
            dma((3,)), dma((2,)),
            dma((3, 3, 4, CHUNKS)), dma((3, 3, 4, CHUNKS)), dma((3, 3, 4, CHUNKS)), dma((3, 3, 4, CHUNKS)),
            dma((3, 3)), dma((3, 3)), dma((3 * CHUNKS, 3)), dma((3 * CHUNKS, 3)),
            dma((16,)), dma((16,)), dma((2, 3)), dma((2, 3)),
        ],
        compiler_params=pltpu.CompilerParams(
            collective_id=0, has_side_effects=True, vmem_limit_bytes=62 * 1024 * 1024
        ),
        name="mixer",
    )(
        inputs[0], output_grad[0], norm_gain[None], gate_bias[None], state_in,
        w_gate.reshape(halves), w_cand.reshape(halves), w_out.reshape(halves),
    )
    part = pl.BlockSpec((TOKENS, BLOCK), lambda n: (0, n))
    short = pl.BlockSpec((1, 32), lambda n: (0, 0))
    layer, grad, state_grad, bias_grad = pl.pallas_call(
        restore_kernel,
        out_shape=(
            jax.ShapeDtypeStruct((TOKENS, WIDTH), BF16),
            jax.ShapeDtypeStruct((TOKENS, WIDTH), BF16),
            jax.ShapeDtypeStruct((1, 32), F32),
            jax.ShapeDtypeStruct((1, 32), F32),
        ),
        grid=(WIDTH // BLOCK,),
        in_specs=[part, part, short, short],
        out_specs=[part, part, short, short],
        name="restore",
    )(layer, grad, state_grad, bias_grad)
    return (layer[None], grad[None], state_grad, bias_grad[0])


def solution(mesh):
    return jax.shard_map(
        on_device,
        mesh=mesh,
        in_specs=(
            P("batch", "seq", None),
            P("batch", "seq", None),
            P(),
            P("seq"),
            P("batch", "seq"),
            P("seq", None),
            P("seq", None),
            P("seq", None),
        ),
        out_specs=(P("batch", "seq", None), P("batch", "seq", None), P("batch", "seq"), P("seq")),
        check_vma=False,
    )
```

```python
import jax
import jax.numpy as jnp
from jax import lax
from jax.sharding import PartitionSpec as P
from jax.experimental import pallas as pl
from jax.experimental.pallas import tpu as pltpu

EPSILON = 1e-06
MESH = pl.DeviceIdType.MESH
ORDERS = ("xyz", "yzx", "zxy")
AXIS_DIM = {"z": 0, "x": 1, "y": 2}
CHUNKS = 4
TOKENS = 256
WIDTH = 2048
SPAN = WIDTH // CHUNKS
BLOCK = 512
STEPS = TOKENS // 8
UNROLL = 32
LANES = 512
F32 = jnp.float32
BF16 = jnp.bfloat16
NT = (((1,), (1,)), ((), ()))


class Place:
    def __init__(self):
        seq = lax.axis_index("seq")
        batch = lax.axis_index("batch")
        self.seq, self.batch = seq, batch
        self.at = {"z": seq // 16, "x": lax.rem(seq // 4, 4), "y": lax.rem(seq, 4)}
        self.z_hi = batch // 2
        self.core = lax.rem(batch, 2)

    def device(self, z, x, y, z_hi, core):
        return (z * 16 + x * 4 + y, z_hi * 2 + core)

    def line(self, axis, step):
        at = dict(self.at)
        at[axis] = lax.rem(at[axis] + 4 + step, 4)
        return self.device(at["z"], at["x"], at["y"], self.z_hi, self.core)

    def column(self, step, flip):
        full = lax.rem(self.z_hi * 4 + self.at["z"] + 8 + step, 8)
        core = lax.rem(self.core + flip, 2)
        return self.device(lax.rem(full, 4), self.at["x"], self.at["y"], full // 4, core)

    def ring(self, axis, step):
        return self.column(step, 0) if axis == "z" else self.line(axis, step)

    def sibling(self):
        return self.column(0, 1)


def remote(src, dst, send_sem, recv_sem, device):
    return pltpu.make_async_remote_copy(
        src_ref=src, dst_ref=dst, send_sem=send_sem, recv_sem=recv_sem, device_id=device, device_id_type=MESH
    )


class Weights:
    def __init__(self, place, buffer, send_sem, recv_sem, sib_send, sib_recv):
        self.place, self.buffer = place, buffer
        self.sems, self.sib_sems = (send_sem, recv_sem), (sib_send, sib_recv)

    def slab(self, w, phase, step, which, q, part, prev=None):
        index = [None, None, None]
        for position, axis in enumerate(ORDERS[w]):
            own_at = self.place.at[axis]
            if position == phase - 1 and prev is not None:
                index[AXIS_DIM[axis]] = lax.rem(own_at + 4 + prev, 4)
            elif position < phase:
                index[AXIS_DIM[axis]] = slice(None)
            elif position == phase:
                index[AXIS_DIM[axis]] = lax.rem(own_at + 4 + step, 4)
            else:
                index[AXIS_DIM[axis]] = own_at
        start, width = 0, WIDTH
        if phase == 2 and w == 0:
            index[AXIS_DIM["x"]] = q
        elif phase == 2:
            start, width = q * SPAN, SPAN
        if part is not None:
            width = width // 2
            start = start + part * width
        return self.buffer.at[w, index[0], index[1], index[2], which, :, pl.ds(start, width)]

    def piece(self, w, phase, kind, q, which, outgoing):
        right = kind % 2 == 0
        if kind < 2:
            step, part = (0 if outgoing else (-1 if right else 1)), None
        else:
            step, part = ((-1 if right else 1) if outgoing else 2), kind - 2
        return self.slab(w, phase, step, which, q, part)

    def copy(self, ref, w, phase, kind, q):
        device = self.place.ring(ORDERS[w][phase], 1 if kind % 2 == 0 else -1)
        at = (w, phase, kind, q)
        return remote(ref, ref, self.sems[0].at[at], self.sems[1].at[at], device)

    def hop(self, w, phase, kind, q, outgoing):
        return self.copy(self.piece(w, phase, kind, q, self.place.core, outgoing), w, phase, kind, q)

    def share(self, w, phase, kind, q, mine):
        ref = self.piece(w, phase, kind, q, self.place.core if mine else 1 - self.place.core, False)
        at = (w, phase, kind, q)
        return remote(ref, ref, self.sib_sems[0].at[at], self.sib_sems[1].at[at], self.place.sibling())

    def part(self, w, phase, q, prev):
        for kind in (0, 1):
            self.copy(self.slab(w, phase, 0, self.place.core, q, None, prev), w, phase, kind, q).start()

    def open(self):
        for w in range(3):
            for kind in (0, 1):
                self.hop(w, 0, kind, 0, True).start()
        for w in range(3):
            self.part(w, 1, 0, 0)

    def near(self, phase, q):
        ahead = {0: (0,), 1: (0,), 2: ()}[phase]
        for w in range(3):
            for kind in (0, 1):
                self.hop(w, phase, kind, q, False).wait_recv()
                self.hop(w, phase, kind + 2, q, True).start()
                self.share(w, phase, kind, q, True).start()
                for later in ahead:
                    self.part(w, phase + 1, later, 1 if kind else -1)

    def far(self, phase, q):
        for w in range(3):
            for kind in (2, 3):
                self.hop(w, phase, kind, q, False).wait_recv()
                self.share(w, phase, kind, q, True).start()
            if phase == 0:
                self.part(w, 1, 0, 2)
            if phase == 1:
                self.part(w, 2, 0, 2)
        if phase == 0:
            for later in (0, 1):
                for w in range(3):
                    self.part(w, 2, later, 0)

    def rest(self, q, prevs):
        for w in range(3):
            for prev in prevs:
                self.part(w, 2, q, prev)

    def shared(self, w, phase, q):
        for kind in range(4):
            self.share(w, phase, kind, q, False).wait_recv()

    def drain(self, phase, q):
        for w in range(3):
            for kind in range(4):
                self.hop(w, phase, kind, q, True).wait_send()
                self.share(w, phase, kind, q, True).wait_send()


class LineExchange:
    def __init__(self, place, axis, ref_of, send_sem, recv_sem, level):
        self.place, self.axis, self.ref_of = place, axis, ref_of
        self.sems, self.level = (send_sem, recv_sem), level

    def copy(self, step, outgoing):
        at = self.place.at[self.axis]
        ref = self.ref_of(at if outgoing else lax.rem(at + 4 - step, 4))
        sem = (self.level, step - 1)
        return remote(ref, ref, self.sems[0].at[sem], self.sems[1].at[sem], self.place.line(self.axis, step))

    def start(self):
        for step in (1, 2, 3):
            self.copy(step, True).start()

    def arrive(self):
        for step in (1, 2, 3):
            self.copy(step, False).wait_recv()

    def drain(self):
        for step in (1, 2, 3):
            self.copy(step, True).wait_send()


def kernel(
    x_hbm, g_hbm, gain_ref, bias_ref, state_ref, gate_w, cand_w, out_w,
    layer_ref, grad_ref, state_grad_ref, bias_grad_ref,
    weights, smalls, pair, x_in, g_in, x_p, g_p, normed, inverse, retain, update, cand, back, factor,
    states, gate_g, cand_g, layer_acc, grad_acc, seg_keep, seg_end, seg_carry, enter, leave, sums, vectors, bias_acc,
    red0, red_in, red_x, red_y,
    own_sem, in_sem, send_sem, recv_sem, sib_send, sib_recv, small_send, small_recv, sum_send, sum_recv,
    red_send, red_recv, last_send, last_recv,
):
    place = Place()
    z, x, y = place.at["z"], place.at["x"], place.at["y"]
    barrier = pltpu.get_barrier_semaphore()
    column_peers = [(dz, dc) for dz in range(8) for dc in range(2) if dz or dc]
    peers = [place.line(a, d) for a in "xy" for d in (1, 2, 3)]
    peers += [place.column(dz, dc) for dz, dc in column_peers]
    for peer in peers:
        pl.semaphore_signal(barrier, inc=1, device_id=peer, device_id_type=MESH)

    read_x = pltpu.make_async_copy(x_hbm, x_in, in_sem.at[0])
    read_g = pltpu.make_async_copy(g_hbm, g_in, in_sem.at[1])
    own = [pltpu.make_async_copy(w, weights.at[k, z, x, y], own_sem.at[k]) for k, w in enumerate((out_w, gate_w, cand_w))]
    read_x.start()
    own[0].start()
    for k, w in ((1, gate_w), (2, cand_w)):
        for q in range(4):
            for i in range(4):
                pltpu.make_async_copy(
                    w.at[:, :, pl.ds((i * 4 + q) * 128, 128)],
                    weights.at[k, z, x, y, :, :, pl.ds((q * 4 + i) * 128, 128)],
                    own_sem.at[k],
                ).start()
    read_g.start()
    lane = lax.broadcasted_iota(jnp.int32, (2, 128), 1)
    small = [jnp.concatenate([ref[...]] * 4, axis=1) for ref in (bias_ref, state_ref)]
    smalls[z, x, y] = jnp.where(lane // 32 == y, jnp.concatenate(small, axis=0), 0.0)

    gather = Weights(place, weights, send_sem, recv_sem, sib_send, sib_recv)
    small_lines = [
        LineExchange(place, "y", lambda v: smalls.at[z, x, v], small_send, small_recv, 0),
        LineExchange(place, "x", lambda v: smalls.at[z, v], small_send, small_recv, 1),
        LineExchange(place, "z", lambda v: smalls.at[v], small_send, small_recv, 2),
    ]

    def blocks(body):
        @pl.loop(0, WIDTH // BLOCK)
        def _(n):
            body(pl.ds(pl.multiple_of(n * BLOCK, BLOCK), BLOCK), n)

    row = lax.broadcasted_iota(jnp.int32, (TOKENS, TOKENS), 0)
    column = lax.broadcasted_iota(jnp.int32, (TOKENS, TOKENS), 1)
    permute = jnp.where(column == lax.rem(row, 8) * STEPS + row // 8, 1.0, 0.0).astype(BF16)
    inverse[...] = jnp.zeros_like(inverse)

    def prepare(cols, n):
        rows = jnp.dot(permute, x_in[:, cols], preferred_element_type=F32)
        x_p[:, cols] = rows.astype(BF16)
        inverse[...] += jnp.sum(rows * rows, axis=1, keepdims=True)

    def prepare_grads(cols, n):
        g_p[:, cols] = jnp.dot(permute, g_in[:, cols], preferred_element_type=F32).astype(BF16)

    def normalise(cols, n):
        normed[:, cols] = (x_p[:, cols].astype(F32) * inverse[...] * gain_ref[:, cols]).astype(BF16)

    read_x.wait()
    blocks(prepare)
    inverse[...] = lax.rsqrt(inverse[...] * (1.0 / WIDTH) + EPSILON)
    for copy in own:
        copy.wait()
    pl.semaphore_wait(barrier, len(peers))

    small_lines[0].start()
    gather.open()
    read_g.wait()
    blocks(prepare_grads)
    small_lines[0].arrive()
    small_lines[1].start()
    gather.near(0, 0)
    gather.far(0, 0)
    blocks(normalise)
    small_lines[1].arrive()
    small_lines[2].start()
    gather.near(1, 0)
    gather.far(1, 0)
    gather.rest(1, (-1,))

    def gather_pair():
        small_lines[2].arrive()
        for i in range(4):
            for j in range(4):
                pair[:, pl.ds((4 * j + i) * 128, 128)] = (
                    smalls[i, j, 0] + smalls[i, j, 1] + smalls[i, j, 2] + smalls[i, j, 3]
                )

    def stage_gates(q):
        gather.shared(1, 2, q)
        gather.shared(2, 2, q)
        lanes = pl.ds(q * SPAN, SPAN)
        for w, dst in ((1, retain), (2, cand)):
            block = weights[w, :, :, :, :, :, lanes].reshape(WIDTH, SPAN)
            dst[:, lanes] = jnp.dot(normed[...], block, preferred_element_type=F32).astype(BF16).astype(F32)

    def forward_scan(q):
        lanes = pl.ds(q * SPAN, SPAN)
        bias = pair[0:1, lanes]

        def step(i, carry):
            reach, state = carry
            rows = pl.ds(pl.multiple_of(i * 8, 8), 8)
            gate = retain[rows, lanes] + bias
            fade = jnp.exp(-jnp.abs(gate))
            high = 1.0 / (1.0 + fade)
            low = fade * high
            up = gate >= 0.0
            u = jnp.where(up, high, low)
            r = jnp.where(up, low, high)
            update[rows, lanes] = u
            retain[rows, lanes] = r
            return reach * r, r * state + u * cand[rows, lanes]

        start = (jnp.ones((8, SPAN), F32), jnp.zeros((8, SPAN), F32))
        reach, state = lax.fori_loop(0, STEPS, step, start, unroll=UNROLL)
        seg_keep[:, lanes] = reach
        seg_end[:, lanes] = state

    def stage_back(q):
        gather.shared(0, 2, q)
        block = weights[0, :, q].reshape(SPAN, WIDTH)
        rows = lax.dot_general(g_p[...], block, NT, preferred_element_type=F32)
        back[:, pl.ds(q * SPAN, SPAN)] = rows.astype(BF16).astype(F32)

    def backward_scan(q):
        lanes = pl.ds(q * SPAN, SPAN)

        def step(i, carry):
            rows = pl.ds(pl.multiple_of((STEPS - 1 - i) * 8, 8), 8)
            return retain[rows, lanes] * (back[rows, lanes] + carry)

        seg_carry[:, lanes] = lax.fori_loop(0, STEPS, step, jnp.zeros((8, SPAN), F32), unroll=UNROLL)

    lines = [
        [
            LineExchange(
                place, axis, lambda v, level=level, q=q: sums.at[level, q, v], sum_send, sum_recv, level * CHUNKS + q
            )
            for q in range(CHUNKS)
        ]
        for level, axis in enumerate("yxz")
    ]

    def publish(level, q, total):
        at = place.at["yxz"[level]]
        for k in range(3):
            sums[level, q, at, k : k + 1, :] = total[k]
        lines[level][q].start()

    def summarise(q):
        lanes = pl.ds(q * SPAN, SPAN)
        keeps, ends, carries = seg_keep[:, lanes], seg_end[:, lanes], seg_carry[:, lanes]
        keep, end, carry = keeps[0:1], ends[0:1], carries[7:8]
        for k in range(1, 8):
            end = keeps[k : k + 1] * end + ends[k : k + 1]
            keep = keep * keeps[k : k + 1]
            carry = carries[7 - k : 8 - k] + keeps[7 - k : 8 - k] * carry
        publish(0, q, (keep, end, carry))

    def compose(level, q):
        at = place.at["yxz"[level]]
        lines[level][q].arrive()
        keeps = [sums[level, q, m, 0:1, :] for m in range(4)]
        ends = [sums[level, q, m, 1:2, :] for m in range(4)]
        carries = [sums[level, q, m, 2:3, :] for m in range(4)]
        keep, end, carry = keeps[0], ends[0], carries[3]
        for m in range(1, 4):
            end = keeps[m] * end + ends[m]
            keep = keep * keeps[m]
            carry = carries[3 - m] + keeps[3 - m] * carry
        if level < 2:
            publish(level + 1, q, (keep, end, carry))
        else:
            vectors[q, 12] = carry
        one, zero = jnp.ones((1, SPAN), F32), jnp.zeros((1, SPAN), F32)
        before, arrived, after, returned = one, zero, one, zero
        for m in range(3):
            take = m < at
            arrived = jnp.where(take, keeps[m] * arrived + ends[m], arrived)
            before = jnp.where(take, keeps[m] * before, before)
        for m in (3, 2, 1):
            take = m > at
            returned = jnp.where(take, carries[m] + keeps[m] * returned, returned)
            after = jnp.where(take, keeps[m] * after, after)
        for k, value in enumerate((before, arrived, after, returned)):
            vectors[q, 4 * level + k] = value

    def settle(q):
        lanes = pl.ds(q * SPAN, SPAN)
        entering, leaving = pair[1:2, lanes], jnp.zeros((1, SPAN), F32)
        for level in (2, 1, 0):
            entering = vectors[q, 4 * level] * entering + vectors[q, 4 * level + 1]
            leaving = vectors[q, 4 * level + 2] * leaving + vectors[q, 4 * level + 3]
        keeps, ends, carries = seg_keep[:, lanes], seg_end[:, lanes], seg_carry[:, lanes]
        for k in range(8):
            enter[k : k + 1, lanes] = entering
            leave[7 - k : 8 - k, lanes] = leaving
            if k < 7:
                entering = keeps[k : k + 1] * entering + ends[k : k + 1]
                leaving = keeps[7 - k : 8 - k] * leaving + carries[7 - k : 8 - k]

    def gradients(q):
        lanes = pl.ds(q * SPAN, SPAN)

        def ahead(i, state):
            halves = []
            for k in range(2):
                rows = pl.ds(pl.multiple_of(i * 16 + k * 8, 8), 8)
                r, u, c = retain[rows, lanes], update[rows, lanes], cand[rows, lanes]
                factor[rows, lanes] = (c - state) * u * r
                state = r * state + u * c
                halves.append(state)
            states[pl.ds(pl.multiple_of(i * 16, 16), 16), lanes] = jnp.concatenate(halves, axis=0).astype(BF16)
            return state

        lax.fori_loop(0, STEPS // 2, ahead, enter[:, lanes], unroll=2)

        def astern(i, carry):
            coming, total_bias = carry
            gates, cands = [None, None], [None, None]
            for k in (1, 0):
                rows = pl.ds(pl.multiple_of((STEPS // 2 - 1 - i) * 16 + k * 8, 8), 8)
                carried = back[rows, lanes] + coming
                gates[k] = carried * factor[rows, lanes]
                cands[k] = carried * update[rows, lanes]
                coming = retain[rows, lanes] * carried
                total_bias = total_bias + gates[k]
            rows = pl.ds(pl.multiple_of((STEPS // 2 - 1 - i) * 16, 16), 16)
            gate_g[rows, lanes] = jnp.concatenate(gates, axis=0).astype(BF16)
            cand_g[rows, lanes] = jnp.concatenate(cands, axis=0).astype(BF16)
            return coming, total_bias

        start = (leave[:, lanes], jnp.zeros((8, SPAN), F32))
        _, total_bias = lax.fori_loop(0, STEPS // 2, astern, start, unroll=2)
        bias_acc[:, lanes] = jnp.sum(total_bias, axis=0, keepdims=True)
        for i in range(4):
            red0[i, q : q + 1, :] = bias_acc[:, pl.ds((4 * q + i) * 128, 128)]

    def layer_part(q, cols):
        block = weights[0, :, q, :, :, :, cols].reshape(SPAN, BLOCK)
        return jnp.dot(states[:, pl.ds(q * SPAN, SPAN)], block, preferred_element_type=F32)

    def grad_part(q, n):
        lanes = pl.ds(q * SPAN, SPAN)
        rows = None
        for w, value in ((1, gate_g), (2, cand_g)):
            block = weights[w, n, :, :, :, :, lanes].reshape(BLOCK, SPAN)
            term = lax.dot_general(value[:, lanes], block, NT, preferred_element_type=F32)
            rows = term if rows is None else rows + term
        return rows

    def accumulate_layer(q):
        def body(cols, n):
            layer_acc[:, cols] = layer_part(q, cols) + (layer_acc[:, cols] if q else x_p[:, cols].astype(F32))

        blocks(body)

    def accumulate_grad(q):
        def body(cols, n):
            grad_acc[:, cols] = grad_part(q, n) + (grad_acc[:, cols] if q else 0.0)

        blocks(body)

    def poll(q):
        if q == 1:
            for w in range(3):
                for phase in range(2):
                    gather.shared(w, phase, 0)
        if 0 <= q < CHUNKS:
            gather.near(2, q)
            if q + 1 < CHUNKS:
                gather.rest(q + 1, (1, 2))
            if q + 2 < CHUNKS:
                gather.rest(q + 2, (0, -1))
        if 1 <= q <= CHUNKS:
            gather.far(2, q - 1)

    last = CHUNKS - 1
    poll(0)
    for t in range(CHUNKS + 3):
        if t < CHUNKS:
            poll(t + 1)
            stage_gates(t)
            if t == 0:
                gather_pair()
            forward_scan(t)
            stage_back(t)
            backward_scan(t)
            summarise(t)
        for level in range(3):
            if 0 <= t - 1 - level < CHUNKS:
                compose(level, t - 1 - level)
        if t >= 3:
            settle(t - 3)
            gradients(t - 3)
            if t - 3 < last:
                accumulate_layer(t - 3)
            if t - 3 < last - 1:
                accumulate_grad(t - 3)

    def reduce_copy(dz, dc):
        k = dz * 2 + dc
        return remote(
            red0.at[lax.rem(z + dz, 4)], red_in.at[k], red_send.at[k], red_recv.at[k], place.column(dz, dc)
        )

    for dz, dc in column_peers:
        reduce_copy(dz, dc).start()
    accumulate_grad(last - 1)

    own_lanes = pl.ds(pl.multiple_of(z * 128, 128), 128)
    turn = lax.rem(128 - 32 * y, 128)
    state_grad_ref[...] = pltpu.roll(vectors[x, 12, :, own_lanes], turn, 1)[:, :32]

    inverse_rows = inverse[...]

    def unit_block(n, row_sum):
        cols = pl.ds(pl.multiple_of(n * BLOCK, BLOCK), BLOCK)
        rows = (grad_part(last, n) + grad_acc[:, cols]) * gain_ref[:, cols]
        grad_acc[:, cols] = rows
        unit = x_p[:, cols].astype(F32) * inverse_rows
        return row_sum + jnp.sum(rows * unit, axis=1, keepdims=True)

    row_sum = lax.fori_loop(0, WIDTH // BLOCK, unit_block, jnp.zeros((TOKENS, 1), F32))
    mean = row_sum * (1.0 / WIDTH)

    for dz, dc in column_peers:
        reduce_copy(dz, dc).wait_recv()
    part = red0[z]
    for dz, dc in column_peers:
        part = part + red_in[dz * 2 + dc]
    for j in range(4):
        red_x[0, j] = part[j : j + 1, :]

    def copy_x(step):
        return remote(
            red_x.at[0, lax.rem(x + step, 4)], red_x.at[step, 0], last_send.at[0, step - 1],
            last_recv.at[0, step - 1], place.line("x", step),
        )

    for step in (1, 2, 3):
        copy_x(step).start()

    def finish_layer(cols, n):
        rows = layer_part(last, cols) + layer_acc[:, cols]
        layer_ref[:, cols] = rows.astype(BF16)

    blocks(finish_layer)

    for step in (1, 2, 3):
        copy_x(step).wait_recv()
    red_y[y] = red_x[0, x] + red_x[1, 0] + red_x[2, 0] + red_x[3, 0]
    last_line = LineExchange(place, "y", lambda v: red_y.at[v], last_send, last_recv, 1)
    last_line.start()

    def finish_grad(cols, n):
        unit = x_p[:, cols].astype(F32) * inverse_rows
        rows = g_p[:, cols].astype(F32) + inverse_rows * (grad_acc[:, cols] - unit * mean)
        grad_ref[:, cols] = rows.astype(BF16)

    blocks(finish_grad)

    for phase in range(3):
        for q in range(CHUNKS if phase == 2 else 1):
            gather.drain(phase, q)
    for line in small_lines + lines[0] + lines[1] + lines[2]:
        line.drain()
    for dz, dc in column_peers:
        reduce_copy(dz, dc).wait_send()
    for step in (1, 2, 3):
        copy_x(step).wait_send()
    last_line.arrive()
    bias_total = red_y[0] + red_y[1] + red_y[2] + red_y[3]
    bias_grad_ref[...] = pltpu.roll(bias_total, turn, 1)[:, :32]
    last_line.drain()


def restore_kernel(
    layer_ref, grad_ref, small0_ref, small1_ref, layer_out, grad_out, small0_out, small1_out,
    layer_in, grad_in, layer_rows, grad_rows, in_sem, out_sem,
):
    blocks = range(WIDTH // BLOCK)
    pieces = ((layer_ref, layer_in, layer_rows, layer_out), (grad_ref, grad_in, grad_rows, grad_out))

    def take(k, n):
        cols = pl.ds(n * BLOCK, BLOCK)
        return pltpu.make_async_copy(pieces[k][0].at[:, cols], pieces[k][1].at[:, cols], in_sem.at[k, n])

    def give(k, n):
        cols = pl.ds(n * BLOCK, BLOCK)
        return pltpu.make_async_copy(pieces[k][2].at[:, cols], pieces[k][3].at[:, cols], out_sem.at[k, n])

    order = [(k, n) for k in range(2) for n in blocks]
    for k, n in order:
        take(k, n).start()
    row = lax.broadcasted_iota(jnp.int32, (TOKENS, TOKENS), 0)
    column = lax.broadcasted_iota(jnp.int32, (TOKENS, TOKENS), 1)
    restore = jnp.where(row == lax.rem(column, 8) * STEPS + column // 8, 1.0, 0.0).astype(BF16)
    small0_out[...] = small0_ref[...]
    small1_out[...] = small1_ref[...]
    for k, n in order:
        take(k, n).wait()
        cols = pl.ds(n * BLOCK, BLOCK)
        rows = jnp.dot(restore, pieces[k][1][:, cols], preferred_element_type=F32)
        pieces[k][2][:, cols] = rows.astype(BF16)
        give(k, n).start()
    for k, n in order:
        give(k, n).wait()


def on_device(inputs, output_grad, norm_gain, gate_bias, state_in, w_gate, w_cand, w_out):
    whole = lambda rows, dtype: pltpu.VMEM((rows, WIDTH), dtype)
    dma = pltpu.SemaphoreType.DMA
    anywhere, vmem = pl.BlockSpec(memory_space=pl.ANY), pl.BlockSpec(memory_space=pltpu.VMEM)
    halves = (2, 16, WIDTH)
    layer, grad, state_grad, bias_grad = pl.pallas_call(
        kernel,
        out_shape=(
            jax.ShapeDtypeStruct((TOKENS, WIDTH), BF16),
            jax.ShapeDtypeStruct((TOKENS, WIDTH), BF16),
            jax.ShapeDtypeStruct((1, 32), F32),
            jax.ShapeDtypeStruct((1, 32), F32),
        ),
        in_specs=[anywhere, anywhere, vmem, vmem, vmem, anywhere, anywhere, anywhere],
        out_specs=[vmem] * 4,
        scratch_shapes=[
            pltpu.VMEM((3, 4, 4, 4, 2, 16, WIDTH), BF16),
            pltpu.VMEM((4, 4, 4, 2, 128), F32),
            whole(2, F32),
            whole(TOKENS, BF16), whole(TOKENS, BF16),
            whole(TOKENS, BF16), whole(TOKENS, BF16), whole(TOKENS, BF16),
            pltpu.VMEM((TOKENS, 1), F32),
            whole(TOKENS, F32), whole(TOKENS, F32), whole(TOKENS, F32), whole(TOKENS, F32), whole(TOKENS, F32),
            whole(TOKENS, BF16), whole(TOKENS, BF16), whole(TOKENS, BF16),
            whole(TOKENS, F32), whole(TOKENS, F32),
            whole(8, F32), whole(8, F32), whole(8, F32), whole(8, F32), whole(8, F32),
            pltpu.VMEM((3, CHUNKS, 4, 4, SPAN), F32),
            pltpu.VMEM((CHUNKS, 13, 1, SPAN), F32),
            whole(1, F32),
            pltpu.VMEM((4, 4, 128), F32),
            pltpu.VMEM((16, 4, 128), F32),
            pltpu.VMEM((4, 4, 1, 128), F32),
            pltpu.VMEM((4, 1, 128), F32),
            dma((3,)), dma((2,)),
            dma((3, 3, 4, CHUNKS)), dma((3, 3, 4, CHUNKS)), dma((3, 3, 4, CHUNKS)), dma((3, 3, 4, CHUNKS)),
            dma((3, 3)), dma((3, 3)), dma((3 * CHUNKS, 3)), dma((3 * CHUNKS, 3)),
            dma((16,)), dma((16,)), dma((2, 3)), dma((2, 3)),
        ],
        compiler_params=pltpu.CompilerParams(
            collective_id=0, has_side_effects=True, vmem_limit_bytes=62 * 1024 * 1024
        ),
        name="mixer",
    )(
        inputs[0], output_grad[0], norm_gain[None], gate_bias[None], state_in,
        w_gate.reshape(halves), w_cand.reshape(halves), w_out.reshape(halves),
    )
    layer, grad, state_grad, bias_grad = pl.pallas_call(
        restore_kernel,
        out_shape=(
            jax.ShapeDtypeStruct((TOKENS, WIDTH), BF16),
            jax.ShapeDtypeStruct((TOKENS, WIDTH), BF16),
            jax.ShapeDtypeStruct((1, 32), F32),
            jax.ShapeDtypeStruct((1, 32), F32),
        ),
        in_specs=[anywhere, anywhere, vmem, vmem],
        out_specs=[anywhere, anywhere, vmem, vmem],
        scratch_shapes=[whole(TOKENS, BF16)] * 4 + [dma((2, WIDTH // BLOCK))] * 2,
        name="restore",
    )(layer, grad, state_grad, bias_grad)
    return (layer[None], grad[None], state_grad, bias_grad[0])


def solution(mesh):
    return jax.shard_map(
        on_device,
        mesh=mesh,
        in_specs=(
            P("batch", "seq", None),
            P("batch", "seq", None),
            P(),
            P("seq"),
            P("batch", "seq"),
            P("seq", None),
            P("seq", None),
            P("seq", None),
        ),
        out_specs=(P("batch", "seq", None), P("batch", "seq", None), P("batch", "seq"), P("seq")),
        check_vma=False,
    )
```

```python
import jax
import jax.numpy as jnp
from jax import lax
from jax.sharding import PartitionSpec as P
from jax.experimental import pallas as pl
from jax.experimental.pallas import tpu as pltpu

EPSILON = 1e-06
MESH = pl.DeviceIdType.MESH
ORDERS = ("xyz", "yzx", "zxy")
AXIS_DIM = {"z": 0, "x": 1, "y": 2}
CHUNKS = 4
TOKENS = 256
WIDTH = 2048
SPAN = WIDTH // CHUNKS
BLOCK = 512
STEPS = TOKENS // 8
UNROLL = 32
LANES = 512
F32 = jnp.float32
BF16 = jnp.bfloat16
NT = (((1,), (1,)), ((), ()))


class Place:
    def __init__(self):
        seq = lax.axis_index("seq")
        batch = lax.axis_index("batch")
        self.seq, self.batch = seq, batch
        self.at = {"z": seq // 16, "x": lax.rem(seq // 4, 4), "y": lax.rem(seq, 4)}
        self.z_hi = batch // 2
        self.core = lax.rem(batch, 2)

    def device(self, z, x, y, z_hi, core):
        return (z * 16 + x * 4 + y, z_hi * 2 + core)

    def line(self, axis, step):
        at = dict(self.at)
        at[axis] = lax.rem(at[axis] + 4 + step, 4)
        return self.device(at["z"], at["x"], at["y"], self.z_hi, self.core)

    def column(self, step, flip):
        full = lax.rem(self.z_hi * 4 + self.at["z"] + 8 + step, 8)
        core = lax.rem(self.core + flip, 2)
        return self.device(lax.rem(full, 4), self.at["x"], self.at["y"], full // 4, core)

    def ring(self, axis, step):
        return self.column(step, 0) if axis == "z" else self.line(axis, step)

    def sibling(self):
        return self.column(0, 1)


def remote(src, dst, send_sem, recv_sem, device):
    return pltpu.make_async_remote_copy(
        src_ref=src, dst_ref=dst, send_sem=send_sem, recv_sem=recv_sem, device_id=device, device_id_type=MESH
    )


class Weights:
    def __init__(self, place, buffer, send_sem, recv_sem, sib_send, sib_recv):
        self.place, self.buffer = place, buffer
        self.sems, self.sib_sems = (send_sem, recv_sem), (sib_send, sib_recv)

    def slab(self, w, phase, step, which, q, part, prev=None):
        index = [None, None, None]
        for position, axis in enumerate(ORDERS[w]):
            own_at = self.place.at[axis]
            if position == phase - 1 and prev is not None:
                index[AXIS_DIM[axis]] = lax.rem(own_at + 4 + prev, 4)
            elif position < phase:
                index[AXIS_DIM[axis]] = slice(None)
            elif position == phase:
                index[AXIS_DIM[axis]] = lax.rem(own_at + 4 + step, 4)
            else:
                index[AXIS_DIM[axis]] = own_at
        start, width = 0, WIDTH
        if phase == 2 and w == 0:
            index[AXIS_DIM["x"]] = q
        elif phase == 2:
            start, width = q * SPAN, SPAN
        if part is not None:
            width = width // 2
            start = start + part * width
        return self.buffer.at[w, index[0], index[1], index[2], which, :, pl.ds(start, width)]

    def piece(self, w, phase, kind, q, which, outgoing):
        right = kind % 2 == 0
        if kind < 2:
            step, part = (0 if outgoing else (-1 if right else 1)), None
        else:
            step, part = ((-1 if right else 1) if outgoing else 2), kind - 2
        return self.slab(w, phase, step, which, q, part)

    def copy(self, ref, w, phase, kind, q):
        device = self.place.ring(ORDERS[w][phase], 1 if kind % 2 == 0 else -1)
        at = (w, phase, kind, q)
        return remote(ref, ref, self.sems[0].at[at], self.sems[1].at[at], device)

    def hop(self, w, phase, kind, q, outgoing):
        return self.copy(self.piece(w, phase, kind, q, self.place.core, outgoing), w, phase, kind, q)

    def share(self, w, phase, kind, q, mine):
        ref = self.piece(w, phase, kind, q, self.place.core if mine else 1 - self.place.core, False)
        at = (w, phase, kind, q)
        return remote(ref, ref, self.sib_sems[0].at[at], self.sib_sems[1].at[at], self.place.sibling())

    def part(self, w, phase, q, prev):
        for kind in (0, 1):
            self.copy(self.slab(w, phase, 0, self.place.core, q, None, prev), w, phase, kind, q).start()

    def open(self):
        for w in range(3):
            for kind in (0, 1):
                self.hop(w, 0, kind, 0, True).start()
        for w in range(3):
            self.part(w, 1, 0, 0)

    def near(self, phase, q):
        ahead = {0: (0,), 1: (0,), 2: ()}[phase]
        for w in range(3):
            for kind in (0, 1):
                self.hop(w, phase, kind, q, False).wait_recv()
                self.hop(w, phase, kind + 2, q, True).start()
                self.share(w, phase, kind, q, True).start()
                for later in ahead:
                    self.part(w, phase + 1, later, 1 if kind else -1)

    def far(self, phase, q):
        for w in range(3):
            for kind in (2, 3):
                self.hop(w, phase, kind, q, False).wait_recv()
                self.share(w, phase, kind, q, True).start()
            if phase == 0:
                self.part(w, 1, 0, 2)
            if phase == 1:
                self.part(w, 2, 0, 2)
        if phase == 0:
            for later in (0, 1):
                for w in range(3):
                    self.part(w, 2, later, 0)

    def rest(self, q, prevs):
        for w in range(3):
            for prev in prevs:
                self.part(w, 2, q, prev)

    def shared(self, w, phase, q):
        for kind in range(4):
            self.share(w, phase, kind, q, False).wait_recv()

    def drain(self, phase, q):
        for w in range(3):
            for kind in range(4):
                self.hop(w, phase, kind, q, True).wait_send()
                self.share(w, phase, kind, q, True).wait_send()


class LineExchange:
    def __init__(self, place, axis, ref_of, send_sem, recv_sem, level):
        self.place, self.axis, self.ref_of = place, axis, ref_of
        self.sems, self.level = (send_sem, recv_sem), level

    def copy(self, step, outgoing):
        at = self.place.at[self.axis]
        ref = self.ref_of(at if outgoing else lax.rem(at + 4 - step, 4))
        sem = (self.level, step - 1)
        return remote(ref, ref, self.sems[0].at[sem], self.sems[1].at[sem], self.place.line(self.axis, step))

    def start(self):
        for step in (1, 2, 3):
            self.copy(step, True).start()

    def arrive(self):
        for step in (1, 2, 3):
            self.copy(step, False).wait_recv()

    def drain(self):
        for step in (1, 2, 3):
            self.copy(step, True).wait_send()


def kernel(
    x_hbm, g_hbm, gain_ref, bias_ref, state_ref, gate_w, cand_w, out_w,
    layer_ref, grad_ref, state_grad_ref, bias_grad_ref,
    weights, smalls, pair, x_in, g_in, x_p, g_p, normed, inverse, retain, update, cand, back, factor,
    states, gate_g, cand_g, layer_acc, grad_acc, seg_keep, seg_end, seg_carry, enter, leave, sums, vectors, bias_acc,
    red0, red_in, red_x, red_y,
    own_sem, in_sem, send_sem, recv_sem, sib_send, sib_recv, small_send, small_recv, sum_send, sum_recv,
    red_send, red_recv, last_send, last_recv,
):
    place = Place()
    z, x, y = place.at["z"], place.at["x"], place.at["y"]
    barrier = pltpu.get_barrier_semaphore()
    column_peers = [(dz, dc) for dz in range(8) for dc in range(2) if dz or dc]
    peers = [place.line(a, d) for a in "xy" for d in (1, 3)]
    peers += [place.column(dz, dc) for dz, dc in ((1, 0), (7, 0), (0, 1))]
    for peer in peers:
        pl.semaphore_signal(barrier, inc=1, device_id=peer, device_id_type=MESH)

    read_x = pltpu.make_async_copy(x_hbm, x_in, in_sem.at[0])
    read_g = pltpu.make_async_copy(g_hbm, g_in, in_sem.at[1])
    own = [pltpu.make_async_copy(w, weights.at[k, z, x, y], own_sem.at[k]) for k, w in enumerate((out_w, gate_w, cand_w))]
    read_x.start()
    own[0].start()
    for k, w in ((1, gate_w), (2, cand_w)):
        for q in range(4):
            for i in range(4):
                pltpu.make_async_copy(
                    w.at[:, :, pl.ds((i * 4 + q) * 128, 128)],
                    weights.at[k, z, x, y, :, :, pl.ds((q * 4 + i) * 128, 128)],
                    own_sem.at[k],
                ).start()
    read_g.start()
    lane = lax.broadcasted_iota(jnp.int32, (2, 128), 1)
    small = [jnp.concatenate([ref[...]] * 4, axis=1) for ref in (bias_ref, state_ref)]
    smalls[z, x, y] = jnp.where(lane // 32 == y, jnp.concatenate(small, axis=0), 0.0)

    gather = Weights(place, weights, send_sem, recv_sem, sib_send, sib_recv)
    small_lines = [
        LineExchange(place, "y", lambda v: smalls.at[z, x, v], small_send, small_recv, 0),
        LineExchange(place, "x", lambda v: smalls.at[z, v], small_send, small_recv, 1),
        LineExchange(place, "z", lambda v: smalls.at[v], small_send, small_recv, 2),
    ]

    def blocks(body):
        @pl.loop(0, WIDTH // BLOCK)
        def _(n):
            body(pl.ds(pl.multiple_of(n * BLOCK, BLOCK), BLOCK), n)

    row = lax.broadcasted_iota(jnp.int32, (TOKENS, TOKENS), 0)
    column = lax.broadcasted_iota(jnp.int32, (TOKENS, TOKENS), 1)
    permute = jnp.where(column == lax.rem(row, 8) * STEPS + row // 8, 1.0, 0.0).astype(BF16)
    inverse[...] = jnp.zeros_like(inverse)

    def prepare(cols, n):
        rows = jnp.dot(permute, x_in[:, cols], preferred_element_type=F32)
        x_p[:, cols] = rows.astype(BF16)
        inverse[...] += jnp.sum(rows * rows, axis=1, keepdims=True)

    def prepare_grads(cols, n):
        g_p[:, cols] = jnp.dot(permute, g_in[:, cols], preferred_element_type=F32).astype(BF16)

    def normalise(cols, n):
        normed[:, cols] = (x_p[:, cols].astype(F32) * inverse[...] * gain_ref[:, cols]).astype(BF16)

    read_x.wait()
    blocks(prepare)
    inverse[...] = lax.rsqrt(inverse[...] * (1.0 / WIDTH) + EPSILON)
    for copy in own:
        copy.wait()
    pl.semaphore_wait(barrier, len(peers))

    gather.open()
    read_g.wait()
    blocks(prepare_grads)
    gather.near(0, 0)
    gather.far(0, 0)
    small_lines[0].start()
    blocks(normalise)
    gather.near(1, 0)
    small_lines[0].arrive()
    small_lines[1].start()
    gather.far(1, 0)
    gather.rest(1, (-1,))

    def gather_pair():
        small_lines[2].arrive()
        for i in range(4):
            for j in range(4):
                pair[:, pl.ds((4 * j + i) * 128, 128)] = (
                    smalls[i, j, 0] + smalls[i, j, 1] + smalls[i, j, 2] + smalls[i, j, 3]
                )

    def stage_gates(q):
        gather.shared(1, 2, q)
        gather.shared(2, 2, q)
        lanes = pl.ds(q * SPAN, SPAN)
        for w, dst in ((1, retain), (2, cand)):
            block = weights[w, :, :, :, :, :, lanes].reshape(WIDTH, SPAN)
            dst[:, lanes] = jnp.dot(normed[...], block, preferred_element_type=F32).astype(BF16).astype(F32)

    def forward_scan(q):
        lanes = pl.ds(q * SPAN, SPAN)
        bias = pair[0:1, lanes]

        def step(i, carry):
            reach, state = carry
            rows = pl.ds(pl.multiple_of(i * 8, 8), 8)
            gate = retain[rows, lanes] + bias
            fade = jnp.exp(-jnp.abs(gate))
            high = 1.0 / (1.0 + fade)
            low = fade * high
            up = gate >= 0.0
            u = jnp.where(up, high, low)
            r = jnp.where(up, low, high)
            update[rows, lanes] = u
            retain[rows, lanes] = r
            return reach * r, r * state + u * cand[rows, lanes]

        start = (jnp.ones((8, SPAN), F32), jnp.zeros((8, SPAN), F32))
        reach, state = lax.fori_loop(0, STEPS, step, start, unroll=UNROLL)
        seg_keep[:, lanes] = reach
        seg_end[:, lanes] = state

    def stage_back(q):
        gather.shared(0, 2, q)
        block = weights[0, :, q].reshape(SPAN, WIDTH)
        rows = lax.dot_general(g_p[...], block, NT, preferred_element_type=F32)
        back[:, pl.ds(q * SPAN, SPAN)] = rows.astype(BF16).astype(F32)

    def backward_scan(q):
        lanes = pl.ds(q * SPAN, SPAN)

        def step(i, carry):
            rows = pl.ds(pl.multiple_of((STEPS - 1 - i) * 8, 8), 8)
            return retain[rows, lanes] * (back[rows, lanes] + carry)

        seg_carry[:, lanes] = lax.fori_loop(0, STEPS, step, jnp.zeros((8, SPAN), F32), unroll=UNROLL)

    lines = [
        [
            LineExchange(
                place, axis, lambda v, level=level, q=q: sums.at[level, q, v], sum_send, sum_recv, level * CHUNKS + q
            )
            for q in range(CHUNKS)
        ]
        for level, axis in enumerate("yxz")
    ]

    def publish(level, q, total):
        at = place.at["yxz"[level]]
        for k in range(3):
            sums[level, q, at, k : k + 1, :] = total[k]
        lines[level][q].start()

    def summarise(q):
        lanes = pl.ds(q * SPAN, SPAN)
        keeps, ends, carries = seg_keep[:, lanes], seg_end[:, lanes], seg_carry[:, lanes]
        keep, end, carry = keeps[0:1], ends[0:1], carries[7:8]
        for k in range(1, 8):
            end = keeps[k : k + 1] * end + ends[k : k + 1]
            keep = keep * keeps[k : k + 1]
            carry = carries[7 - k : 8 - k] + keeps[7 - k : 8 - k] * carry
        publish(0, q, (keep, end, carry))

    def compose(level, q):
        at = place.at["yxz"[level]]
        lines[level][q].arrive()
        keeps = [sums[level, q, m, 0:1, :] for m in range(4)]
        ends = [sums[level, q, m, 1:2, :] for m in range(4)]
        carries = [sums[level, q, m, 2:3, :] for m in range(4)]
        keep, end, carry = keeps[0], ends[0], carries[3]
        for m in range(1, 4):
            end = keeps[m] * end + ends[m]
            keep = keep * keeps[m]
            carry = carries[3 - m] + keeps[3 - m] * carry
        if level < 2:
            publish(level + 1, q, (keep, end, carry))
        else:
            vectors[q, 12] = carry
        one, zero = jnp.ones((1, SPAN), F32), jnp.zeros((1, SPAN), F32)
        before, arrived, after, returned = one, zero, one, zero
        for m in range(3):
            take = m < at
            arrived = jnp.where(take, keeps[m] * arrived + ends[m], arrived)
            before = jnp.where(take, keeps[m] * before, before)
        for m in (3, 2, 1):
            take = m > at
            returned = jnp.where(take, carries[m] + keeps[m] * returned, returned)
            after = jnp.where(take, keeps[m] * after, after)
        for k, value in enumerate((before, arrived, after, returned)):
            vectors[q, 4 * level + k] = value

    def settle(q):
        lanes = pl.ds(q * SPAN, SPAN)
        entering, leaving = pair[1:2, lanes], jnp.zeros((1, SPAN), F32)
        for level in (2, 1, 0):
            entering = vectors[q, 4 * level] * entering + vectors[q, 4 * level + 1]
            leaving = vectors[q, 4 * level + 2] * leaving + vectors[q, 4 * level + 3]
        keeps, ends, carries = seg_keep[:, lanes], seg_end[:, lanes], seg_carry[:, lanes]
        for k in range(8):
            enter[k : k + 1, lanes] = entering
            leave[7 - k : 8 - k, lanes] = leaving
            if k < 7:
                entering = keeps[k : k + 1] * entering + ends[k : k + 1]
                leaving = keeps[7 - k : 8 - k] * leaving + carries[7 - k : 8 - k]

    def gradients(q):
        lanes = pl.ds(q * SPAN, SPAN)

        def ahead(i, state):
            halves = []
            for k in range(2):
                rows = pl.ds(pl.multiple_of(i * 16 + k * 8, 8), 8)
                r, u, c = retain[rows, lanes], update[rows, lanes], cand[rows, lanes]
                factor[rows, lanes] = (c - state) * u * r
                state = r * state + u * c
                halves.append(state)
            states[pl.ds(pl.multiple_of(i * 16, 16), 16), lanes] = jnp.concatenate(halves, axis=0).astype(BF16)
            return state

        lax.fori_loop(0, STEPS // 2, ahead, enter[:, lanes], unroll=2)

        def astern(i, carry):
            coming, total_bias = carry
            gates, cands = [None, None], [None, None]
            for k in (1, 0):
                rows = pl.ds(pl.multiple_of((STEPS // 2 - 1 - i) * 16 + k * 8, 8), 8)
                carried = back[rows, lanes] + coming
                gates[k] = carried * factor[rows, lanes]
                cands[k] = carried * update[rows, lanes]
                coming = retain[rows, lanes] * carried
                total_bias = total_bias + gates[k]
            rows = pl.ds(pl.multiple_of((STEPS // 2 - 1 - i) * 16, 16), 16)
            gate_g[rows, lanes] = jnp.concatenate(gates, axis=0).astype(BF16)
            cand_g[rows, lanes] = jnp.concatenate(cands, axis=0).astype(BF16)
            return coming, total_bias

        start = (leave[:, lanes], jnp.zeros((8, SPAN), F32))
        _, total_bias = lax.fori_loop(0, STEPS // 2, astern, start, unroll=2)
        bias_acc[:, lanes] = jnp.sum(total_bias, axis=0, keepdims=True)
        for i in range(4):
            red0[i, q : q + 1, :] = bias_acc[:, pl.ds((4 * q + i) * 128, 128)]

    def layer_part(q, cols):
        block = weights[0, :, q, :, :, :, cols].reshape(SPAN, BLOCK)
        return jnp.dot(states[:, pl.ds(q * SPAN, SPAN)], block, preferred_element_type=F32)

    def grad_part(q, n):
        lanes = pl.ds(q * SPAN, SPAN)
        rows = None
        for w, value in ((1, gate_g), (2, cand_g)):
            block = weights[w, n, :, :, :, :, lanes].reshape(BLOCK, SPAN)
            term = lax.dot_general(value[:, lanes], block, NT, preferred_element_type=F32)
            rows = term if rows is None else rows + term
        return rows

    def accumulate_layer(q):
        def body(cols, n):
            layer_acc[:, cols] = layer_part(q, cols) + (layer_acc[:, cols] if q else x_p[:, cols].astype(F32))

        blocks(body)

    def accumulate_grad(q):
        def body(cols, n):
            grad_acc[:, cols] = grad_part(q, n) + (grad_acc[:, cols] if q else 0.0)

        blocks(body)

    def poll(q):
        if q == 1:
            small_lines[1].arrive()
            small_lines[2].start()
        if q == 1:
            for w in range(3):
                for phase in range(2):
                    gather.shared(w, phase, 0)
        if 0 <= q < CHUNKS:
            gather.near(2, q)
            if q + 1 < CHUNKS:
                gather.rest(q + 1, (1, 2))
            if q + 2 < CHUNKS:
                gather.rest(q + 2, (0, -1))
        if 1 <= q <= CHUNKS:
            gather.far(2, q - 1)

    last = CHUNKS - 1
    poll(0)
    for t in range(CHUNKS + 3):
        if t < CHUNKS:
            poll(t + 1)
            stage_gates(t)
            if t == 0:
                gather_pair()
            forward_scan(t)
            stage_back(t)
            backward_scan(t)
            summarise(t)
        for level in range(3):
            if 0 <= t - 1 - level < CHUNKS:
                compose(level, t - 1 - level)
        if t >= 3:
            settle(t - 3)
            gradients(t - 3)
            if t - 3 < last:
                accumulate_layer(t - 3)
            if t - 3 < last - 1:
                accumulate_grad(t - 3)

    def reduce_copy(dz, dc):
        k = dz * 2 + dc
        return remote(
            red0.at[lax.rem(z + dz, 4)], red_in.at[k], red_send.at[k], red_recv.at[k], place.column(dz, dc)
        )

    for dz, dc in column_peers:
        reduce_copy(dz, dc).start()
    accumulate_grad(last - 1)

    own_lanes = pl.ds(pl.multiple_of(z * 128, 128), 128)
    turn = lax.rem(128 - 32 * y, 128)
    state_grad_ref[...] = pltpu.roll(vectors[x, 12, :, own_lanes], turn, 1)[:, :32]

    inverse_rows = inverse[...]

    def unit_block(n, row_sum):
        cols = pl.ds(pl.multiple_of(n * BLOCK, BLOCK), BLOCK)
        rows = (grad_part(last, n) + grad_acc[:, cols]) * gain_ref[:, cols]
        grad_acc[:, cols] = rows
        unit = x_p[:, cols].astype(F32) * inverse_rows
        return row_sum + jnp.sum(rows * unit, axis=1, keepdims=True)

    row_sum = lax.fori_loop(0, WIDTH // BLOCK, unit_block, jnp.zeros((TOKENS, 1), F32))
    mean = row_sum * (1.0 / WIDTH)

    for dz, dc in column_peers:
        reduce_copy(dz, dc).wait_recv()
    part = red0[z]
    for dz, dc in column_peers:
        part = part + red_in[dz * 2 + dc]
    for j in range(4):
        red_x[0, j] = part[j : j + 1, :]

    def copy_x(step):
        return remote(
            red_x.at[0, lax.rem(x + step, 4)], red_x.at[step, 0], last_send.at[0, step - 1],
            last_recv.at[0, step - 1], place.line("x", step),
        )

    for step in (1, 2, 3):
        copy_x(step).start()

    def finish_layer(cols, n):
        rows = layer_part(last, cols) + layer_acc[:, cols]
        layer_ref[:, cols] = rows.astype(BF16)

    blocks(finish_layer)

    for step in (1, 2, 3):
        copy_x(step).wait_recv()
    red_y[y] = red_x[0, x] + red_x[1, 0] + red_x[2, 0] + red_x[3, 0]
    last_line = LineExchange(place, "y", lambda v: red_y.at[v], last_send, last_recv, 1)
    last_line.start()

    def finish_grad(cols, n):
        unit = x_p[:, cols].astype(F32) * inverse_rows
        rows = g_p[:, cols].astype(F32) + inverse_rows * (grad_acc[:, cols] - unit * mean)
        grad_ref[:, cols] = rows.astype(BF16)

    blocks(finish_grad)

    for phase in range(3):
        for q in range(CHUNKS if phase == 2 else 1):
            gather.drain(phase, q)
    for line in small_lines + lines[0] + lines[1] + lines[2]:
        line.drain()
    for dz, dc in column_peers:
        reduce_copy(dz, dc).wait_send()
    for step in (1, 2, 3):
        copy_x(step).wait_send()
    last_line.arrive()
    bias_total = red_y[0] + red_y[1] + red_y[2] + red_y[3]
    bias_grad_ref[...] = pltpu.roll(bias_total, turn, 1)[:, :32]
    last_line.drain()


def restore_kernel(
    layer_ref, grad_ref, small0_ref, small1_ref, layer_out, grad_out, small0_out, small1_out,
    layer_in, grad_in, layer_rows, grad_rows, in_sem, out_sem,
):
    blocks = range(WIDTH // BLOCK)
    pieces = ((layer_ref, layer_in, layer_rows, layer_out), (grad_ref, grad_in, grad_rows, grad_out))

    def take(k, n):
        cols = pl.ds(n * BLOCK, BLOCK)
        return pltpu.make_async_copy(pieces[k][0].at[:, cols], pieces[k][1].at[:, cols], in_sem.at[k, n])

    def give(k, n):
        cols = pl.ds(n * BLOCK, BLOCK)
        return pltpu.make_async_copy(pieces[k][2].at[:, cols], pieces[k][3].at[:, cols], out_sem.at[k, n])

    order = [(k, n) for k in range(2) for n in blocks]
    for k, n in order:
        take(k, n).start()
    row = lax.broadcasted_iota(jnp.int32, (TOKENS, TOKENS), 0)
    column = lax.broadcasted_iota(jnp.int32, (TOKENS, TOKENS), 1)
    restore = jnp.where(row == lax.rem(column, 8) * STEPS + column // 8, 1.0, 0.0).astype(BF16)
    small0_out[...] = small0_ref[...]
    small1_out[...] = small1_ref[...]
    for k, n in order:
        take(k, n).wait()
        cols = pl.ds(n * BLOCK, BLOCK)
        rows = jnp.dot(restore, pieces[k][1][:, cols], preferred_element_type=F32)
        pieces[k][2][:, cols] = rows.astype(BF16)
        give(k, n).start()
    for k, n in order:
        give(k, n).wait()


def on_device(inputs, output_grad, norm_gain, gate_bias, state_in, w_gate, w_cand, w_out):
    whole = lambda rows, dtype: pltpu.VMEM((rows, WIDTH), dtype)
    dma = pltpu.SemaphoreType.DMA
    anywhere, vmem = pl.BlockSpec(memory_space=pl.ANY), pl.BlockSpec(memory_space=pltpu.VMEM)
    halves = (2, 16, WIDTH)
    layer, grad, state_grad, bias_grad = pl.pallas_call(
        kernel,
        out_shape=(
            jax.ShapeDtypeStruct((TOKENS, WIDTH), BF16),
            jax.ShapeDtypeStruct((TOKENS, WIDTH), BF16),
            jax.ShapeDtypeStruct((1, 32), F32),
            jax.ShapeDtypeStruct((1, 32), F32),
        ),
        in_specs=[anywhere, anywhere, vmem, vmem, vmem, anywhere, anywhere, anywhere],
        out_specs=[vmem] * 4,
        scratch_shapes=[
            pltpu.VMEM((3, 4, 4, 4, 2, 16, WIDTH), BF16),
            pltpu.VMEM((4, 4, 4, 2, 128), F32),
            whole(2, F32),
            whole(TOKENS, BF16), whole(TOKENS, BF16),
            whole(TOKENS, BF16), whole(TOKENS, BF16), whole(TOKENS, BF16),
            pltpu.VMEM((TOKENS, 1), F32),
            whole(TOKENS, F32), whole(TOKENS, F32), whole(TOKENS, F32), whole(TOKENS, F32), whole(TOKENS, F32),
            whole(TOKENS, BF16), whole(TOKENS, BF16), whole(TOKENS, BF16),
            whole(TOKENS, F32), whole(TOKENS, F32),
            whole(8, F32), whole(8, F32), whole(8, F32), whole(8, F32), whole(8, F32),
            pltpu.VMEM((3, CHUNKS, 4, 4, SPAN), F32),
            pltpu.VMEM((CHUNKS, 13, 1, SPAN), F32),
            whole(1, F32),
            pltpu.VMEM((4, 4, 128), F32),
            pltpu.VMEM((16, 4, 128), F32),
            pltpu.VMEM((4, 4, 1, 128), F32),
            pltpu.VMEM((4, 1, 128), F32),
            dma((3,)), dma((2,)),
            dma((3, 3, 4, CHUNKS)), dma((3, 3, 4, CHUNKS)), dma((3, 3, 4, CHUNKS)), dma((3, 3, 4, CHUNKS)),
            dma((3, 3)), dma((3, 3)), dma((3 * CHUNKS, 3)), dma((3 * CHUNKS, 3)),
            dma((16,)), dma((16,)), dma((2, 3)), dma((2, 3)),
        ],
        compiler_params=pltpu.CompilerParams(
            collective_id=0, has_side_effects=True, vmem_limit_bytes=62 * 1024 * 1024
        ),
        name="mixer",
    )(
        inputs[0], output_grad[0], norm_gain[None], gate_bias[None], state_in,
        w_gate.reshape(halves), w_cand.reshape(halves), w_out.reshape(halves),
    )
    layer, grad, state_grad, bias_grad = pl.pallas_call(
        restore_kernel,
        out_shape=(
            jax.ShapeDtypeStruct((TOKENS, WIDTH), BF16),
            jax.ShapeDtypeStruct((TOKENS, WIDTH), BF16),
            jax.ShapeDtypeStruct((1, 32), F32),
            jax.ShapeDtypeStruct((1, 32), F32),
        ),
        in_specs=[anywhere, anywhere, vmem, vmem],
        out_specs=[anywhere, anywhere, vmem, vmem],
        scratch_shapes=[whole(TOKENS, BF16)] * 4 + [dma((2, WIDTH // BLOCK))] * 2,
        name="restore",
    )(layer, grad, state_grad, bias_grad)
    return (layer[None], grad[None], state_grad, bias_grad[0])


def solution(mesh):
    return jax.shard_map(
        on_device,
        mesh=mesh,
        in_specs=(
            P("batch", "seq", None),
            P("batch", "seq", None),
            P(),
            P("seq"),
            P("batch", "seq"),
            P("seq", None),
            P("seq", None),
            P("seq", None),
        ),
        out_specs=(P("batch", "seq", None), P("batch", "seq", None), P("batch", "seq"), P("seq")),
        check_vma=False,
    )
```
